512 devices in a mesh: lat: 64 (over y_lo, z, core), tgt: 8 (over y_hi, x).
Axes of the slice: x: 4, y: 8 (y_hi: 2, y_lo: 4; y = y_hi * 4 + y_lo), z: 8, core: 2. Of those that a mesh axis runs over, the one named last changes fastest.
Arguments:
- inputs: bfloat16 [512, 2, 2304], P('lat', None, 'tgt'), may hold values from -6 to 6
- w_enc: bfloat16 [2304, 32768], P('tgt', 'lat'), may hold values from -0.125 to 0.125
- b_enc: float32 [32768], P('lat'), may hold values from -4 to 4
- masks: int32 [512, 32768], P(None, 'lat'), may hold values 0 or 1
- w_dec: bfloat16 [8, 32768, 2304], P('tgt', 'lat'), may hold values from -0.046875 to 0.046875
- errors: bfloat16 [8, 512, 2304], P('tgt', 'lat'), may hold values from -6 to 6
- target_of: int32 [8], replicated, may hold values from 0 to 7, each once
Outputs:
- grad_enc: float32 [2304, 32768], P('tgt', 'lat')
- grad_bias: float32 [32768], P('lat')
- grad_in: float32 [512, 2, 2304], P('lat', None, 'tgt')
The draws below stay inside these ranges and needn't reach their ends.
Inputs may be any that keep to these rules, and one draw needn't show every extreme that they name: `target_of`: each target layer names exactly one slot.
All inputs are finite; a program needn't handle non-finite values. No bound on the sum of `masks` on one device may be relied on, other than what follows from the above.
Results may differ from the reference program's by a relative error of at most 0.0029.
Values may be sent and summed in bfloat16 or wider, within the bound.
No kernel may reach another device: no remote copies, remote signals or barrier semaphores. Data moves between devices by JAX's collectives and lax.ppermute only.
A program may use at most 64 MiB of HBM per device.

```python
import jax
import jax.numpy as jnp
from jax import lax

D = 2304
F = 16384
S = 2
TOKENS = 512
LATS = 32768
TGT = 8


def touch_ends(values, key, smallest, top_value):
    dims = values.shape
    spot = [jax.random.randint(jax.random.fold_in(key, axis), (), 0, dims[axis]) for axis in range(len(dims))]
    values = values.at[tuple(spot)].set(smallest)
    longest = dims.index(max(dims))
    spot[longest] = (spot[longest] + 1) % dims[longest]
    return values.at[tuple(spot)].set(top_value)


def shard_levels(key, shape, shards, low, largest):
    level = 1.0
    for axis_at, blocks in shards:
        steps = jax.random.uniform(jax.random.fold_in(jax.random.fold_in(key, 6), axis_at), (blocks,), jnp.float32, low / len(shards), largest / len(shards))
        level = level * jnp.repeat(jnp.exp(steps), shape[axis_at] // blocks).reshape((-1,) + (1,) * (len(shape) - 1 - axis_at))
    return level


def centred(stream_key, shape, width, bound, split=(), held_as=jnp.bfloat16):
    factor_of = shard_levels(stream_key, shape, split, -0.22, 0.18) if split else 1.0
    result = jax.random.normal(stream_key, shape, jnp.float32) * width * factor_of
    return jnp.minimum(jnp.maximum(result, -bound), bound).astype(held_as)


def setup_inputs(seed: int = 0) -> dict:
    arg_keys = jax.random.split(jax.random.key(seed), 8)
    inputs = centred(arg_keys[0], (TOKENS, S, D), 1.0, 6.0, ((0, 64), (2, 8)))
    w_enc = centred(arg_keys[1], (D, LATS), D ** -0.5, 0.125, ((0, 8), (1, 64)))
    b_enc = centred(arg_keys[2], (LATS,), 1.0, 4.0, ((0, 64),), jnp.float32)
    masks = touch_ends((jax.random.randint(arg_keys[3], (TOKENS, LATS), 0, 4) < 1).astype(jnp.int32), jax.random.fold_in(arg_keys[3], 1), 0, 1)
    w_dec = centred(arg_keys[4], (TGT, LATS, D), F ** -0.5, 0.046875, ((0, 8), (1, 64)))
    errors = centred(arg_keys[5], (TGT, TOKENS, D), 1.0, 6.0, ((0, 8), (1, 64)))
    target_of = jax.random.permutation(arg_keys[6], TGT).astype(jnp.int32)
    return dict(inputs=inputs, w_enc=w_enc, b_enc=b_enc, masks=masks, w_dec=w_dec, errors=errors, target_of=target_of)


penalty = 1.0
sharpness = 1.0

def reference(inputs, w_enc, b_enc, masks, w_dec, errors, target_of):
    source = jnp.arange(LATS, dtype=jnp.int32) // F
    live = (target_of[:, None] >= source[None, :]).astype(jnp.float32)
    pieces = []
    for layer in range(S):
        pieces.append(jnp.dot(inputs[:, layer, :], w_enc[:, layer * F:(layer + 1) * F], preferred_element_type=jnp.float32))
    pre = jnp.concatenate(pieces, axis=1) + b_enc[None, :]
    gates = masks.astype(jnp.float32)
    act = gates * pre
    squares = lax.map(lambda w: lax.optimization_barrier(jnp.sum(jnp.square(w.astype(jnp.float32)), axis=1)), w_dec)
    norm = jnp.sqrt(lax.optimization_barrier(jnp.sum(live * squares, axis=0)))
    dact = jnp.zeros((TOKENS, LATS), jnp.float32)
    for slot in range(TGT):
        dact = dact + live[slot][None, :] * jnp.dot(errors[slot], w_dec[slot].T, preferred_element_type=jnp.float32)
    tanh_val = jnp.tanh(sharpness * act * norm[None, :])
    grad = (gates * (dact + penalty * sharpness * norm[None, :] * (1.0 - tanh_val * tanh_val))).astype(jnp.bfloat16)
    grad_bias = lax.optimization_barrier(jnp.sum(grad.astype(jnp.float32), axis=0))
    enc_parts = []
    in_parts = []
    for layer in range(S):
        cols = grad[:, layer * F:(layer + 1) * F]
        enc_parts.append(jnp.dot(inputs[:, layer, :].T, cols, preferred_element_type=jnp.float32))
        in_parts.append(jnp.dot(cols, w_enc[:, layer * F:(layer + 1) * F].T, preferred_element_type=jnp.float32))
    grad_enc = jnp.concatenate(enc_parts, axis=1)
    grad_in = jnp.stack(in_parts, axis=1)
    return (grad_enc, grad_bias, grad_in)
```

```python
import jax
import jax.numpy as jnp
from jax import lax
from jax.sharding import Mesh, PartitionSpec as P

S = 2
penalty = 1.0
sharpness = 1.0

YL, Z, C, YH, X = 4, 8, 2, 2, 4
AXES = ("yl", "z", "c", "yh", "x")
LAT = ("yl", "z", "c")
TGT = ("yh", "x")
PLANE = ("yl", "z")
PRE_BOUND = 1024.0
SWAP = [(0, 1), (1, 0)]
TOP = 14.0


def exponent(bound):
    return jnp.ceil(jnp.log2(jnp.maximum(bound, 1e-30)))


def split_bf16(v):
    hi = v.astype(jnp.bfloat16)
    rest = v - hi.astype(jnp.float32)
    mid = rest.astype(jnp.bfloat16)
    low = (rest - mid.astype(jnp.float32)).astype(jnp.bfloat16)
    return jnp.stack([hi, mid, low])


def local(inputs, w_enc, b_enc, masks, w_dec, errors, target_of):
    f32, bf16, f16 = jnp.float32, jnp.bfloat16, jnp.float16
    yl, core = lax.axis_index("yl"), lax.axis_index("c")
    x = lax.axis_index("x")
    slot = lax.axis_index("yh") * X + x
    source = yl * S // YL
    feats, lats = w_enc.shape
    depth = w_dec.shape[2]
    rows = inputs.shape[0]
    slots = jnp.arange(target_of.shape[0], dtype=jnp.int32)
    layer = jnp.sum(jnp.where(slots == slot, target_of, 0))
    flag = (layer >= source).astype(f32)

    gates5 = masks.reshape(YL, Z, C, rows, lats)
    gates4 = lax.dynamic_index_in_dim(gates5, x, 0, keepdims=False)
    gates_own = lax.dynamic_index_in_dim(gates4, core, 1, keepdims=False).reshape(Z * rows, lats)
    gates_send = lax.dynamic_index_in_dim(gates4, 1 - core, 1, keepdims=False).reshape(Z * rows, lats)
    w_own = w_dec[0]
    w_other = lax.ppermute(w_own, "c", SWAP)
    pack = jnp.concatenate(
        [w_enc, gates_send.astype(bf16), split_bf16(b_enc), jnp.zeros((13, lats), bf16)], axis=0
    )
    pack_other = lax.ppermute(pack, "c", SWAP)

    top_err = jnp.max(jnp.abs(errors[0].astype(f32))) * 1.01
    parts = []
    for dest in range(YL):
        parts.append(
            jnp.concatenate(
                [
                    errors[0],
                    inputs[:, dest * S // YL, :],
                    jnp.broadcast_to(top_err.astype(bf16), (rows, 96)),
                ],
                axis=1,
            )
        )
    send = jnp.stack(parts)[:, None]
    width = send.shape[-1]
    send = jnp.broadcast_to(send, (YL, Z, rows, width)).reshape(YL * Z, rows, width)
    got = lax.all_to_all(send, PLANE, 0, 0, tiled=True).reshape(YL * Z * rows, width)
    errs, own = got[:, :depth], got[:, depth : depth + feats]
    top_err = jnp.max(got[:, depth + feats : depth + feats + 1].astype(f32))
    wide = got.shape[0]
    chunk = wide // X

    sq_own = jnp.einsum("cd,cd->c", w_own, w_own, preferred_element_type=f32)
    sq_other = jnp.einsum("cd,cd->c", w_other, w_other, preferred_element_type=f32)
    w_enc_other = pack_other[:feats]
    gates_other = pack_other[feats : feats + chunk].astype(f32)
    bias_rows = pack_other[feats + chunk : feats + chunk + 3].astype(f32)
    b_other = bias_rows[0] + bias_rows[1] + bias_rows[2]
    squares = flag * jnp.concatenate([sq_own, sq_other])
    dims = (((1,), (1,)), ((), ()))
    term = jnp.concatenate(
        [
            lax.dot_general(errs, w_own, dims, preferred_element_type=f32),
            lax.dot_general(errs, w_other, dims, preferred_element_type=f32),
        ],
        axis=1,
    )
    partial_pre = jnp.concatenate(
        [
            jnp.dot(own, w_enc, preferred_element_type=f32),
            jnp.dot(own, w_enc_other, preferred_element_type=f32),
        ],
        axis=1,
    )

    top_sq = jnp.max(squares)
    e_term = exponent(jnp.sqrt(depth * 1.01 * top_sq) * top_err)
    e_sq = exponent(top_sq)
    pre_scale = 32768.0 / PRE_BOUND

    def extra_rows(sq, e_sq, e_term):
        scaled = sq * jnp.exp2(TOP - e_sq)
        hi = scaled.astype(f16)
        low = (scaled - hi.astype(f32)).astype(f16)
        line = lambda e: jnp.broadcast_to(e.astype(f16), hi.shape)
        return jnp.concatenate(
            [jnp.stack([hi, low, line(e_sq), line(e_term)]), jnp.zeros((12,) + hi.shape, f16)], axis=0
        )

    extra = extra_rows(squares, e_sq, e_term)
    out = jnp.concatenate(
        [
            (term * (flag * jnp.exp2(TOP - e_term))).astype(f16).reshape(X, chunk, C * lats),
            (partial_pre * pre_scale).astype(f16).reshape(X, chunk, C * lats),
            jnp.broadcast_to(extra[None], (X,) + extra.shape),
        ],
        axis=1,
    )
    back = lax.all_to_all(out, "x", 0, 0, tiled=True)

    def decode(block):
        e_sq = block[2 * chunk + 2, 0].astype(f32)
        e_term = block[2 * chunk + 3, 0].astype(f32)
        dact = block[:chunk].astype(f32) * jnp.exp2(e_term - TOP)
        pre = block[chunk : 2 * chunk].astype(f32) * (1.0 / pre_scale)
        sq = (block[2 * chunk].astype(f32) + block[2 * chunk + 1].astype(f32)) * jnp.exp2(e_sq - TOP)
        return dact, pre, sq, e_sq, e_term

    dact, pre, sq, es, et = decode(back[0])
    for i in range(1, X):
        d1, p1, s1, es1, et1 = decode(back[i])
        dact, pre, sq = dact + d1, pre + p1, sq + s1
        es, et = jnp.maximum(es, es1), jnp.maximum(et, et1)
    es, et = es + 2.0, et + 2.0
    half = jnp.concatenate(
        [
            (dact * jnp.exp2(TOP - et)).astype(f16),
            (pre * pre_scale).astype(f16),
            extra_rows(sq, es, et),
        ],
        axis=0,
    )
    d1, p1, s1, _, _ = decode(lax.ppermute(half, "yh", SWAP))
    dact, pre, sumsq = dact + d1, pre + p1, sq + s1

    gates = jnp.concatenate([gates_own.astype(f32), gates_other], axis=1)
    pre = pre + jnp.concatenate([b_enc, b_other])[None, :]
    norm = jnp.sqrt(sumsq)[None, :]
    tanh_val = jnp.tanh(sharpness * (gates * pre) * norm)
    grad = (gates * (dact + penalty * sharpness * norm * (1.0 - tanh_val * tanh_val))).astype(bf16)

    grad = lax.all_to_all(
        jnp.broadcast_to(grad[None], (X,) + grad.shape), "x", 0, 0, tiled=True
    ).reshape(wide, C * lats)
    g_own, g_other = grad[:, :lats], grad[:, lats:]
    rows_dims = (((0,), (0,)), ((), ()))

    def enc(g):
        return lax.dot_general(own, g, rows_dims, preferred_element_type=f32)

    def bias(g):
        return jnp.broadcast_to(jnp.sum(g.astype(f32), axis=0)[None], (8, lats))

    away = lax.ppermute(jnp.concatenate([enc(g_other), bias(g_other)], axis=0), "c", SWAP)

    part = lax.dot_general(g_own, w_enc, dims, preferred_element_type=f32) + lax.dot_general(
        g_other, w_enc_other, dims, preferred_element_type=f32
    )
    e_part = exponent(jnp.max(jnp.abs(part)))
    sent = jnp.concatenate(
        [
            (part * jnp.exp2(TOP - e_part)).astype(f16),
            jnp.broadcast_to(e_part.astype(f16), (wide, 96)),
        ],
        axis=1,
    ).reshape(YL * Z, rows, feats + 96)
    came = lax.all_to_all(sent, PLANE, 0, 0, tiled=True)
    values = came[:, :, :feats].astype(f32) * jnp.exp2(
        came[:, :, feats : feats + 1].astype(f32) - TOP
    )
    sums = jnp.sum(values.reshape(S, YL * Z // S, rows, feats), axis=1)
    grad_in = jnp.transpose(sums, (1, 0, 2))
    grad_enc = enc(g_own) + away[:feats]
    grad_bias = jnp.sum(g_own.astype(f32), axis=0) + away[feats]
    return (grad_enc, grad_bias, grad_in)


def solution(mesh):
    fine = Mesh(mesh.devices.reshape(YL, Z, C, YH, X), AXES)
    return jax.shard_map(
        local,
        mesh=fine,
        in_specs=(
            P(LAT, None, TGT),
            P(TGT, LAT),
            P(LAT),
            P(None, LAT),
            P(TGT, LAT, None),
            P(TGT, LAT, None),
            P(),
        ),
        out_specs=(P(TGT, LAT), P(LAT), P(LAT, None, TGT)),
        check_vma=False,
    )
```

```python
import jax
import jax.numpy as jnp
from jax import lax
from jax.sharding import Mesh, PartitionSpec as P

S = 2
penalty = 1.0
sharpness = 1.0

YL, Z, C, YH, X = 4, 8, 2, 2, 4
AXES = ("yl", "z", "c", "yh", "x")
LAT = ("yl", "z", "c")
TGT = ("yh", "x")
PLANE = ("yl", "z")
SUMS = ("x", "yh")
PEERS = YL * Z
SLOTS = YH * X
LANES = 384
EXTRA = 8
PRE_SCALE = 64.0
TOP = 14.0


def exponent(bound):
    return jnp.ceil(jnp.log2(jnp.maximum(bound, 1e-30)))


def split_bf16(v):
    hi = v.astype(jnp.bfloat16)
    rest = v - hi.astype(jnp.float32)
    mid = rest.astype(jnp.bfloat16)
    low = (rest - mid.astype(jnp.float32)).astype(jnp.bfloat16)
    return jnp.stack([hi, mid, low])


def swap(value, axis, size, distance):
    return lax.ppermute(value, axis, [(i, i ^ distance) for i in range(size)])


def local(inputs, w_enc, b_enc, masks, w_dec, errors, target_of):
    f32, bf16, f16 = jnp.float32, jnp.bfloat16, jnp.float16
    yl, z, core = (lax.axis_index(a) for a in LAT)
    yh, x = lax.axis_index("yh"), lax.axis_index("x")
    place = x * YH + yh
    source = yl * S // YL
    feats, lats = w_enc.shape
    depth = w_dec.shape[2]
    rows = inputs.shape[0]
    wide = PEERS * rows
    chunk = wide // SLOTS
    both_lats = C * lats
    pad = LANES - feats
    dims = (((1,), (1,)), ((), ()))
    rows_dims = (((0,), (0,)), ((), ()))

    errs = lax.all_to_all(
        jnp.broadcast_to(errors, (PEERS, rows, depth)), PLANE, 0, 0, tiled=True
    ).reshape(wide, depth)

    top_err = jnp.max(jnp.abs(errors[0].astype(f32))) * 1.01
    top_lanes = jnp.broadcast_to(top_err.astype(bf16), (rows, S, pad))
    held = jnp.transpose(jnp.concatenate([inputs, top_lanes], axis=2), (1, 0, 2))
    mine = lax.dynamic_index_in_dim(held, source, 0, keepdims=True)
    theirs = swap(lax.dynamic_index_in_dim(held, 1 - source, 0, keepdims=True), "yl", YL, 2)
    low = source == 0
    held = jnp.concatenate([jnp.where(low, mine, theirs), jnp.where(low, theirs, mine)], axis=0)
    for axis, size, at, distance in (("z", Z, z, 1), ("z", Z, z, 2), ("z", Z, z, 4), ("yl", YL, yl, 1)):
        theirs = swap(held, axis, size, distance)
        low = (at & distance) == 0
        held = jnp.concatenate([jnp.where(low, held, theirs), jnp.where(low, theirs, held)], axis=1)
    own = held.reshape(wide, LANES)
    top_err = jnp.max(own[:, feats : feats + 1].astype(f32))
    lane = lax.broadcasted_iota(jnp.int32, (wide, LANES), 1)
    own_ones = jnp.where(lane < feats, own, jnp.ones_like(own))

    gates6 = masks.reshape(SLOTS, chunk // rows, C, rows, lats)
    gates5 = lax.dynamic_index_in_dim(gates6, place, 0, keepdims=False)
    gates_own = lax.dynamic_index_in_dim(gates5, core, 1, keepdims=False).reshape(chunk, lats)
    gates_send = lax.dynamic_index_in_dim(gates5, 1 - core, 1, keepdims=False).reshape(chunk, lats)
    w_own = w_dec[0]
    pack = jnp.concatenate(
        [
            w_enc,
            jnp.zeros((pad, lats), bf16),
            gates_send.astype(bf16),
            split_bf16(b_enc),
            jnp.zeros((13, lats), bf16),
        ],
        axis=0,
    )
    pack_other = swap(pack, "c", C, 1)
    w_other = swap(w_own, "c", C, 1)
    w_both = jnp.concatenate([w_own, w_other], axis=0)
    enc_both = jnp.concatenate([pack[:LANES], pack_other[:LANES]], axis=1)
    gates_other = pack_other[LANES : LANES + chunk].astype(f32)
    gates = jnp.concatenate([gates_own.astype(f32), gates_other], axis=1)
    bias_rows = pack_other[LANES + chunk : LANES + chunk + 3].astype(f32)
    b_both = jnp.concatenate([b_enc, bias_rows[0] + bias_rows[1] + bias_rows[2]])

    slots = jnp.arange(target_of.shape[0], dtype=jnp.int32)
    layer = jnp.sum(jnp.where(slots == yh * X + x, target_of, 0))
    flag = (layer >= source).astype(f32)
    squares = flag * jnp.einsum("cd,cd->c", w_both, w_both, preferred_element_type=f32)

    top_sq = jnp.max(squares)
    e_term = exponent(jnp.sqrt(depth * 1.01 * top_sq) * top_err)
    e_sq = exponent(top_sq)

    def lines(sq, e, tops):
        scaled = sq * jnp.exp2(TOP - e)
        hi = scaled.astype(f16)
        rest = (scaled - hi.astype(f32)).astype(f16)
        table = [hi[None], rest[None], jnp.broadcast_to(e.astype(f16), (1, both_lats)), tops.astype(f16)]
        spare = EXTRA - 3 - tops.shape[0]
        return jnp.concatenate(table + [jnp.zeros((spare, both_lats), f16)], axis=0)

    def unlines(table):
        return (table[0] + table[1]) * jnp.exp2(table[2] - TOP), table[2, 0]

    partial_pre = jnp.dot(own, enc_both, preferred_element_type=f32) * PRE_SCALE
    extra = lines(squares, e_sq, jnp.broadcast_to(e_term, (1, both_lats)))
    pre_out = jnp.concatenate(
        [
            partial_pre.astype(f16).reshape(X, YH * chunk, both_lats),
            jnp.broadcast_to(extra[None], (X, EXTRA, both_lats)),
        ],
        axis=1,
    )
    blocks = [lax.dynamic_index_in_dim(pre_out, x, 0, keepdims=False)]
    for k in range(1, X):
        blocks.append(swap(lax.dynamic_index_in_dim(pre_out, x ^ k, 0, keepdims=False), "x", X, k))
    blocks = [b.astype(f32) for b in blocks]
    pre = sum(b[: YH * chunk] for b in blocks)
    sq, e_sq = 0.0, -100.0
    tops = jnp.zeros((X, both_lats), f32)
    for k in range(X):
        table = blocks[k][YH * chunk :]
        sq_k, e_k = unlines(table)
        sq, e_sq = sq + sq_k, jnp.maximum(e_sq, e_k)
        tops = tops + jnp.where(lax.broadcasted_iota(jnp.int32, (X, 1), 0) == (x ^ k), table[3:4], 0.0)
    pre = pre.reshape(YH, chunk, both_lats)
    half = jnp.concatenate(
        [
            lax.dynamic_index_in_dim(pre, 1 - yh, 0, keepdims=False).astype(f16),
            lines(sq, e_sq + 2.0, tops),
        ],
        axis=0,
    )
    half = swap(half, "yh", YH, 1).astype(f32)
    pre = lax.dynamic_index_in_dim(pre, yh, 0, keepdims=False) + half[:chunk]
    pre = pre * (1.0 / PRE_SCALE) + b_both[None, :]
    sumsq = sq + unlines(half[chunk:])[0]
    tops_far = half[chunk + 3 : chunk + 3 + X]
    first = yh == 0
    tops = jnp.stack([jnp.where(first, tops, tops_far), jnp.where(first, tops_far, tops)], axis=1)
    unscale = jnp.exp2(tops.reshape(SLOTS, 1, both_lats) - TOP)
    norm = jnp.sqrt(sumsq)[None, :]
    tanh_val = jnp.tanh(sharpness * (gates * pre) * norm)
    pull = penalty * sharpness * norm * (1.0 - tanh_val * tanh_val)

    term = lax.dot_general(errs, w_both, dims, preferred_element_type=f32)
    term = (term * (flag * jnp.exp2(TOP - e_term))).astype(f16).reshape(SLOTS, chunk, both_lats)
    terms = lax.all_to_all(term, SUMS, 0, 0, tiled=True)
    dact = jnp.sum(terms.astype(f32) * unscale, axis=0)
    grad = (gates * (dact + pull)).astype(bf16)

    grad = lax.all_to_all(
        jnp.broadcast_to(grad[None], (SLOTS, chunk, both_lats)), SUMS, 0, 0, tiled=True
    ).reshape(wide, both_lats)

    part = lax.dot_general(grad, enc_both, dims, preferred_element_type=f32)
    e_part = exponent(jnp.max(jnp.abs(part)))
    sent = jnp.where(lane < feats, part * jnp.exp2(TOP - e_part), e_part).astype(f16)
    sent, grad = lax.optimization_barrier((sent, grad))
    came = lax.all_to_all(sent.reshape(PEERS, rows, LANES), PLANE, 0, 0, tiled=True)
    came = came.reshape(wide, LANES)

    enc = lax.dot_general(own_ones, grad, rows_dims, preferred_element_type=f32)
    away = swap(enc[: feats + 8, lats:], "c", C, 1)
    grad_enc = enc[:feats, :lats] + away[:feats]
    grad_bias = enc[feats, :lats] + away[feats]

    spread = (lax.broadcasted_iota(jnp.int32, (LANES, feats), 0) == feats).astype(bf16)
    e_rows = jnp.dot(came.astype(bf16), spread, preferred_element_type=f32)
    values = came[:, :feats].astype(f32) * jnp.exp2(e_rows - TOP)
    sums = jnp.sum(values.reshape(S, PEERS // S, rows, feats), axis=1)
    return (grad_enc, grad_bias, jnp.transpose(sums, (1, 0, 2)))


def solution(mesh):
    fine = Mesh(mesh.devices.reshape(YL, Z, C, YH, X), AXES)
    return jax.shard_map(
        local,
        mesh=fine,
        in_specs=(
            P(LAT, None, TGT),
            P(TGT, LAT),
            P(LAT),
            P(None, LAT),
            P(TGT, LAT, None),
            P(TGT, LAT, None),
            P(),
        ),
        out_specs=(P(TGT, LAT), P(LAT), P(LAT, None, TGT)),
        check_vma=False,
    )
```

```python
import jax
import jax.numpy as jnp
from jax import lax
from jax.sharding import Mesh, PartitionSpec as P

S = 2
penalty = 1.0
sharpness = 1.0

YL, Z, C, YH, X = 4, 8, 2, 2, 4
AXES = ("yl", "z", "c", "yh", "x")
LAT = ("yl", "z", "c")
TGT = ("yh", "x")
PLANE = ("yl", "z")
SUMS = ("x", "yh")
PEERS = YL * Z
SLOTS = YH * X
LANES = 384
EXTRA = 8
PRE_SCALE = 64.0
TOP = 14.0


def exponent(bound):
    return jnp.ceil(jnp.log2(jnp.maximum(bound, 1e-30)))


def split_bf16(v):
    hi = v.astype(jnp.bfloat16)
    rest = v - hi.astype(jnp.float32)
    mid = rest.astype(jnp.bfloat16)
    low = (rest - mid.astype(jnp.float32)).astype(jnp.bfloat16)
    return jnp.stack([hi, mid, low])


def swap(value, axis, size, distance):
    return lax.ppermute(value, axis, [(i, i ^ distance) for i in range(size)])


def local(inputs, w_enc, b_enc, masks, w_dec, errors, target_of):
    f32, bf16, f16 = jnp.float32, jnp.bfloat16, jnp.float16
    yl, core = lax.axis_index("yl"), lax.axis_index("c")
    yh, x = lax.axis_index("yh"), lax.axis_index("x")
    place = x * YH + yh
    source = yl * S // YL
    feats, lats = w_enc.shape
    depth = w_dec.shape[2]
    rows = inputs.shape[0]
    wide = PEERS * rows
    chunk = wide // SLOTS
    both_lats = C * lats
    pad = LANES - feats
    dims = (((1,), (1,)), ((), ()))
    rows_dims = (((0,), (0,)), ((), ()))

    top_err = jnp.max(jnp.abs(errors[0].astype(f32))) * 1.01
    top_lanes = jnp.broadcast_to(top_err.astype(bf16), (rows, pad))
    held = [jnp.concatenate([inputs[:, s], top_lanes], axis=1)[None] for s in range(S)]
    held = jnp.concatenate([jnp.broadcast_to(h, (PEERS // S, rows, LANES)) for h in held], axis=0)
    held = lax.all_to_all(held, PLANE, 0, 0, tiled=True)
    errs = lax.all_to_all(
        jnp.broadcast_to(errors, (PEERS, rows, depth)), PLANE, 0, 0, tiled=True
    ).reshape(wide, depth)
    own = held.reshape(wide, LANES)
    top_err = jnp.max(own[:, feats : feats + 1].astype(f32))
    lane = lax.broadcasted_iota(jnp.int32, (wide, LANES), 1)
    own_ones = jnp.where(lane < feats, own, jnp.ones_like(own))

    gates6 = masks.reshape(SLOTS, chunk // rows, C, rows, lats)
    gates5 = lax.dynamic_index_in_dim(gates6, place, 0, keepdims=False)
    gates_own = lax.dynamic_index_in_dim(gates5, core, 1, keepdims=False).reshape(chunk, lats)
    gates_send = lax.dynamic_index_in_dim(gates5, 1 - core, 1, keepdims=False).reshape(chunk, lats)
    w_own = w_dec[0]
    pack = jnp.concatenate(
        [
            w_enc,
            jnp.zeros((pad, lats), bf16),
            gates_send.astype(bf16),
            split_bf16(b_enc),
            jnp.zeros((13, lats), bf16),
        ],
        axis=0,
    )
    pack_other = swap(pack, "c", C, 1)
    w_other = swap(w_own, "c", C, 1)
    w_both = jnp.concatenate([w_own, w_other], axis=0)
    enc_both = jnp.concatenate([pack[:LANES], pack_other[:LANES]], axis=1)
    gates_other = pack_other[LANES : LANES + chunk].astype(f32)
    gates = jnp.concatenate([gates_own.astype(f32), gates_other], axis=1)
    bias_rows = pack_other[LANES + chunk : LANES + chunk + 3].astype(f32)
    b_both = jnp.concatenate([b_enc, bias_rows[0] + bias_rows[1] + bias_rows[2]])

    slots = jnp.arange(target_of.shape[0], dtype=jnp.int32)
    layer = jnp.sum(jnp.where(slots == yh * X + x, target_of, 0))
    flag = (layer >= source).astype(f32)
    squares = flag * jnp.einsum("cd,cd->c", w_both, w_both, preferred_element_type=f32)

    top_sq = jnp.max(squares)
    e_term = exponent(jnp.sqrt(depth * 1.01 * top_sq) * top_err)
    e_sq = exponent(top_sq)

    def lines(sq, e, tops):
        scaled = sq * jnp.exp2(TOP - e)
        hi = scaled.astype(f16)
        rest = (scaled - hi.astype(f32)).astype(f16)
        table = [hi[None], rest[None], jnp.broadcast_to(e.astype(f16), (1, both_lats)), tops.astype(f16)]
        spare = EXTRA - 3 - tops.shape[0]
        return jnp.concatenate(table + [jnp.zeros((spare, both_lats), f16)], axis=0)

    def unlines(table):
        return (table[0] + table[1]) * jnp.exp2(table[2] - TOP), table[2, 0]

    partial_pre = jnp.dot(own, enc_both, preferred_element_type=f32) * PRE_SCALE
    extra = lines(squares, e_sq, jnp.broadcast_to(e_term, (1, both_lats)))
    pre_out = jnp.concatenate(
        [
            partial_pre.astype(f16).reshape(X, YH * chunk, both_lats),
            jnp.broadcast_to(extra[None], (X, EXTRA, both_lats)),
        ],
        axis=1,
    )
    blocks = [lax.dynamic_index_in_dim(pre_out, x, 0, keepdims=False)]
    for k in range(1, X):
        blocks.append(swap(lax.dynamic_index_in_dim(pre_out, x ^ k, 0, keepdims=False), "x", X, k))
    blocks = [b.astype(f32) for b in blocks]
    pre = sum(b[: YH * chunk] for b in blocks)
    sq, e_sq = 0.0, -100.0
    tops = jnp.zeros((X, both_lats), f32)
    for k in range(X):
        table = blocks[k][YH * chunk :]
        sq_k, e_k = unlines(table)
        sq, e_sq = sq + sq_k, jnp.maximum(e_sq, e_k)
        tops = tops + jnp.where(lax.broadcasted_iota(jnp.int32, (X, 1), 0) == (x ^ k), table[3:4], 0.0)
    pre = pre.reshape(YH, chunk, both_lats)
    half = jnp.concatenate(
        [
            lax.dynamic_index_in_dim(pre, 1 - yh, 0, keepdims=False).astype(f16),
            lines(sq, e_sq + 2.0, tops),
        ],
        axis=0,
    )
    half = swap(half, "yh", YH, 1).astype(f32)
    pre = lax.dynamic_index_in_dim(pre, yh, 0, keepdims=False) + half[:chunk]
    pre = pre * (1.0 / PRE_SCALE) + b_both[None, :]
    sumsq = sq + unlines(half[chunk:])[0]
    tops_far = half[chunk + 3 : chunk + 3 + X]
    first = yh == 0
    tops = jnp.stack([jnp.where(first, tops, tops_far), jnp.where(first, tops_far, tops)], axis=1)
    unscale = jnp.exp2(tops.reshape(SLOTS, 1, both_lats) - TOP)
    norm = jnp.sqrt(sumsq)[None, :]
    tanh_val = jnp.tanh(sharpness * (gates * pre) * norm)
    pull = penalty * sharpness * norm * (1.0 - tanh_val * tanh_val)

    term = lax.dot_general(errs, w_both, dims, preferred_element_type=f32)
    term = (term * (flag * jnp.exp2(TOP - e_term))).astype(f16).reshape(SLOTS, chunk, both_lats)
    terms = lax.all_to_all(term, SUMS, 0, 0, tiled=True)
    dact = jnp.sum(terms.astype(f32) * unscale, axis=0)
    grad = (gates * (dact + pull)).astype(bf16)

    grad = lax.all_to_all(
        jnp.broadcast_to(grad[None], (SLOTS, chunk, both_lats)), SUMS, 0, 0, tiled=True
    ).reshape(wide, both_lats)

    part = lax.dot_general(grad, enc_both, dims, preferred_element_type=f32)
    e_part = exponent(jnp.max(jnp.abs(part)))
    sent = jnp.where(lane < feats, part * jnp.exp2(TOP - e_part), e_part).astype(f16)
    sent, grad = lax.optimization_barrier((sent, grad))
    came = lax.all_to_all(sent.reshape(PEERS, rows, LANES), PLANE, 0, 0, tiled=True)
    came = came.reshape(wide, LANES)

    enc = lax.dot_general(own_ones, grad, rows_dims, preferred_element_type=f32)
    away = swap(enc[: feats + 8, lats:], "c", C, 1)
    grad_enc = enc[:feats, :lats] + away[:feats]
    grad_bias = enc[feats, :lats] + away[feats]

    spread = (lax.broadcasted_iota(jnp.int32, (LANES, feats), 0) == feats).astype(bf16)
    e_rows = jnp.dot(came.astype(bf16), spread, preferred_element_type=f32)
    values = came[:, :feats].astype(f32) * jnp.exp2(e_rows - TOP)
    sums = jnp.sum(values.reshape(S, PEERS // S, rows, feats), axis=1)
    return (grad_enc, grad_bias, jnp.transpose(sums, (1, 0, 2)))


def solution(mesh):
    fine = Mesh(mesh.devices.reshape(YL, Z, C, YH, X), AXES)
    return jax.shard_map(
        local,
        mesh=fine,
        in_specs=(
            P(LAT, None, TGT),
            P(TGT, LAT),
            P(LAT),
            P(None, LAT),
            P(TGT, LAT, None),
            P(TGT, LAT, None),
            P(),
        ),
        out_specs=(P(TGT, LAT), P(LAT), P(LAT, None, TGT)),
        check_vma=False,
    )
```

```python
import functools

import jax
import jax.numpy as jnp
from jax import lax
from jax.experimental import pallas as pl
from jax.experimental.pallas import tpu as pltpu
from jax.sharding import Mesh, PartitionSpec as P

S = 2
penalty = 1.0
sharpness = 1.0

YL, Z, C, YH, X = 4, 8, 2, 2, 4
AXES = ("yl", "z", "c", "yh", "x")
LAT = ("yl", "z", "c")
TGT = ("yh", "x")
PLANE = ("yl", "z")
PEERS = YL * Z
SLOTS = YH * X
LANES = 384
EXTRA = 8
PRE_SCALE = 128.0
TOP = 14.0
SWAP = [(0, 1), (1, 0)]
f32, bf16, f16 = jnp.float32, jnp.bfloat16, jnp.float16
BY_LAST = (((1,), (1,)), ((), ()))
BY_FIRST = (((0,), (0,)), ((), ()))
PARAMS = pltpu.CompilerParams(vmem_limit_bytes=40 * 1024 * 1024)


def exponent(bound):
    return jnp.ceil(jnp.log2(jnp.maximum(bound, 1e-30)))


def split_bf16(v):
    hi = v.astype(bf16)
    rest = v - hi.astype(f32)
    mid = rest.astype(bf16)
    low = (rest - mid.astype(f32)).astype(bf16)
    return jnp.stack([hi, mid, low])


def call(body, outs, *args):
    shapes = [jax.ShapeDtypeStruct(*o) for o in outs]
    return pl.pallas_call(body, out_shape=shapes, compiler_params=PARAMS)(*args)


def forward(feats, got, w_own, w_other, enc_both, lines, base, out, ones_out):
    wide = got.shape[0]
    depth = w_own.shape[1]
    lats = w_own.shape[0]
    chunk = wide // SLOTS
    errs = got[:, :depth]
    own = got[:, depth:]
    lane = lax.broadcasted_iota(jnp.int32, own.shape, 1)
    own32 = own.astype(f32)
    ones_out[...] = jnp.where(lane < feats, own32, 1.0).astype(bf16)
    top_err = jnp.max(jnp.where(lane == feats, own32, 0.0), axis=(0, 1), keepdims=True)
    e_term = exponent(base[:, 0:1] * top_err)
    scale = base[:, 1:2] * jnp.exp2(TOP - e_term)
    for h, w in enumerate((w_own, w_other)):
        term = lax.dot_general(errs, w[...], BY_LAST, preferred_element_type=f32) * scale
        out[:, :chunk, h * lats : (h + 1) * lats] = term.reshape(SLOTS, chunk, lats)
    pre = jnp.dot(own, enc_both[...], preferred_element_type=f32) * PRE_SCALE
    out[:, chunk : 2 * chunk, :] = pre.reshape(SLOTS, chunk, C * lats)
    row = lax.broadcasted_iota(jnp.int32, lines.shape, 0)
    extra = jnp.where(row == 3, jnp.broadcast_to(e_term, lines.shape), lines[...])
    for i in range(SLOTS):
        out[i, 2 * chunk :, :] = extra


def middle(back, gates, bias, out):
    chunk = gates.shape[0]
    dact = jnp.zeros(gates.shape, f32)
    pre = jnp.zeros(gates.shape, f32)
    sumsq = jnp.zeros((1, gates.shape[1]), f32)
    at = 2 * chunk
    for i in range(SLOTS):
        dact += back[i, :chunk, :] * jnp.exp2(back[i, at + 3 : at + 4, :] - TOP)
        pre += back[i, chunk:at, :]
        squares = back[i, at : at + 1, :] + back[i, at + 1 : at + 2, :]
        sumsq += squares * jnp.exp2(back[i, at + 2 : at + 3, :] - TOP)
    pre = pre * (1.0 / PRE_SCALE) + bias[...]
    norm = jnp.sqrt(sumsq)
    tanh_val = jnp.tanh(sharpness * (gates[...] * pre) * norm)
    grad = gates[...] * (dact + penalty * sharpness * norm * (1.0 - tanh_val * tanh_val))
    grad = grad.astype(bf16)
    for i in range(SLOTS):
        out[i] = grad


def backward(feats, grad, enc_both, own_ones, sent, keep, away):
    lats = keep.shape[1]
    part = lax.dot_general(grad[...], enc_both[...], BY_LAST, preferred_element_type=f32)
    e_part = exponent(jnp.max(jnp.abs(part), axis=(0, 1), keepdims=True))
    lane = lax.broadcasted_iota(jnp.int32, part.shape, 1)
    sent[...] = jnp.where(lane < feats, part * jnp.exp2(TOP - e_part), jnp.broadcast_to(e_part, part.shape))
    enc = lax.dot_general(own_ones[...], grad[...], BY_FIRST, preferred_element_type=f32)
    keep[...] = enc[: keep.shape[0], :lats]
    away[...] = enc[: away.shape[0], lats:]


def finish(came, keep, far, grad_in, grad_enc, grad_bias):
    rows, _, feats = grad_in.shape
    values = came[:, :feats] * jnp.exp2(came[:, feats : feats + 1] - TOP)
    values = values.reshape(S, PEERS // S, rows, feats)
    for s in range(S):
        grad_in[:, s, :] = jnp.sum(values[s], axis=0)
    both = keep[...] + far[...]
    grad_enc[...] = both[:feats]
    grad_bias[...] = both[feats : feats + 1]


def local(inputs, w_enc, b_enc, masks, w_dec, errors, target_of):
    yl, core = lax.axis_index("yl"), lax.axis_index("c")
    slot = lax.axis_index("yh") * X + lax.axis_index("x")
    source = yl * S // YL
    feats, lats = w_enc.shape
    depth = w_dec.shape[2]
    rows = inputs.shape[0]
    wide = PEERS * rows
    chunk = wide // SLOTS
    both_lats = C * lats
    pad = LANES - feats

    top_err = jnp.max(jnp.abs(errors[0].astype(f32))) * 1.01
    top_lanes = jnp.broadcast_to(top_err.astype(bf16), (rows, pad))
    held = [jnp.concatenate([errors[0], inputs[:, s], top_lanes], axis=1)[None] for s in range(S)]
    held = jnp.concatenate([jnp.broadcast_to(h, (PEERS // S, rows, depth + LANES)) for h in held], axis=0)
    got = lax.all_to_all(held, PLANE, 0, 0, tiled=True).reshape(wide, depth + LANES)

    gates6 = masks.reshape(SLOTS, chunk // rows, C, rows, lats)
    gates5 = lax.dynamic_index_in_dim(gates6, slot, 0, keepdims=False)
    gates_own = lax.dynamic_index_in_dim(gates5, core, 1, keepdims=False).reshape(chunk, lats)
    gates_send = lax.dynamic_index_in_dim(gates5, 1 - core, 1, keepdims=False).reshape(chunk, lats)
    w_own = w_dec[0]
    w_other = lax.ppermute(w_own, "c", SWAP)
    pack = jnp.concatenate(
        [
            w_enc,
            jnp.zeros((pad, lats), bf16),
            gates_send.astype(bf16),
            split_bf16(b_enc),
            jnp.zeros((13, lats), bf16),
        ],
        axis=0,
    )
    pack_other = lax.ppermute(pack, "c", SWAP)
    enc_both = jnp.concatenate([pack[:LANES], pack_other[:LANES]], axis=1)
    gates_other = pack_other[LANES : LANES + chunk].astype(f32)
    gates = jnp.concatenate([gates_own.astype(f32), gates_other], axis=1)
    bias_rows = pack_other[LANES + chunk : LANES + chunk + 3].astype(f32)
    b_both = jnp.concatenate([b_enc, bias_rows[0] + bias_rows[1] + bias_rows[2]])[None]

    slots = jnp.arange(target_of.shape[0], dtype=jnp.int32)
    layer = jnp.sum(jnp.where(slots == slot, target_of, 0))
    flag = (layer >= source).astype(f32)
    square = lambda w: jnp.einsum("cd,cd->c", w, w, preferred_element_type=f32)
    squares = flag * jnp.concatenate([square(w_own), square(w_other)])
    top_sq = jnp.max(squares)
    e_sq = exponent(top_sq)
    scaled = squares * jnp.exp2(TOP - e_sq)
    hi = scaled.astype(f16).astype(f32)
    lines = jnp.concatenate(
        [
            hi[None],
            (scaled - hi)[None],
            jnp.broadcast_to(e_sq, (1, both_lats)),
            jnp.zeros((EXTRA - 3, both_lats), f32),
        ],
        axis=0,
    )
    base = jnp.stack([jnp.sqrt(depth * 1.01 * top_sq), flag])[None]
    lines, base, enc_both, gates, b_both, w_other, got = lax.optimization_barrier(
        (lines, base, enc_both, gates, b_both, w_other, got)
    )

    out, own_ones = call(
        functools.partial(forward, feats),
        [((SLOTS, 2 * chunk + EXTRA, both_lats), f32), ((wide, LANES), bf16)],
        got, w_own, w_other, enc_both, lines, base,
    )
    back = lax.all_to_all(out.astype(f16), TGT, 0, 0, tiled=True).astype(f32)
    (grad,) = call(middle, [((SLOTS, chunk, both_lats), bf16)], back, gates, b_both)
    grad = lax.all_to_all(grad, TGT, 0, 0, tiled=True).reshape(wide, both_lats)
    sent, keep, away = call(
        functools.partial(backward, feats),
        [((wide, LANES), f32), ((feats + 8, lats), f32), ((feats + 8, lats), f32)],
        grad, enc_both, own_ones,
    )
    far = lax.ppermute(away, "c", SWAP)
    came = lax.all_to_all(sent.astype(f16).reshape(PEERS, rows, LANES), PLANE, 0, 0, tiled=True)
    grad_in, grad_enc, grad_bias = call(
        finish,
        [((rows, S, feats), f32), ((feats, lats), f32), ((1, lats), f32)],
        came.astype(f32).reshape(wide, LANES), keep, far,
    )
    return (grad_enc, grad_bias[0], grad_in)


def solution(mesh):
    fine = Mesh(mesh.devices.reshape(YL, Z, C, YH, X), AXES)
    return jax.shard_map(
        local,
        mesh=fine,
        in_specs=(
            P(LAT, None, TGT),
            P(TGT, LAT),
            P(LAT),
            P(None, LAT),
            P(TGT, LAT, None),
            P(TGT, LAT, None),
            P(),
        ),
        out_specs=(P(TGT, LAT), P(LAT), P(LAT, None, TGT)),
        check_vma=False,
    )
```

```python
import functools

import jax
import jax.numpy as jnp
from jax import lax
from jax.experimental import pallas as pl
from jax.experimental.pallas import tpu as pltpu
from jax.sharding import Mesh, PartitionSpec as P

S = 2
penalty = 1.0
sharpness = 1.0

YL, Z, C, YH, X = 4, 8, 2, 2, 4
AXES = ("yl", "z", "c", "yh", "x")
LAT = ("yl", "z", "c")
TGT = ("yh", "x")
PLANE = ("yl", "z")
PEERS = YL * Z
SLOTS = YH * X
LANES = 384
EXTRA = 8
PRE_SCALE = 64.0
TOP = 14.0
SWAP = [(0, 1), (1, 0)]
f32, bf16, f16 = jnp.float32, jnp.bfloat16, jnp.float16
BY_LAST = (((1,), (1,)), ((), ()))
BY_FIRST = (((0,), (0,)), ((), ()))
PARAMS = pltpu.CompilerParams(vmem_limit_bytes=40 * 1024 * 1024)


def exponent(bound):
    return jnp.ceil(jnp.log2(jnp.maximum(bound, 1e-30)))


def split_bf16(v):
    hi = v.astype(bf16)
    rest = v - hi.astype(f32)
    mid = rest.astype(bf16)
    low = (rest - mid.astype(f32)).astype(bf16)
    return jnp.stack([hi, mid, low])


def call(body, outs, *args):
    shapes = [jax.ShapeDtypeStruct(*o) for o in outs]
    return pl.pallas_call(body, out_shape=shapes, compiler_params=PARAMS)(*args)


def prepare(errors, inputs, out):
    rows, depth = errors.shape
    errs = errors[...]
    top_err = jnp.max(jnp.abs(errs.astype(f32)), axis=(0, 1), keepdims=True) * 1.01
    pad = jnp.broadcast_to(top_err, (rows, LANES - inputs.shape[2]))
    for s in range(S):
        last = jnp.concatenate([inputs[:, s, :].astype(f32), pad], axis=1).astype(bf16)
        for i in range(PEERS // S):
            out[s * (PEERS // S) + i, :, :depth] = errs
            out[s * (PEERS // S) + i, :, depth:] = last


def forward(feats, got, w_own, w_other, enc_both, lines, base, out, ones_out):
    wide = got.shape[0]
    depth = w_own.shape[1]
    lats = w_own.shape[0]
    chunk = wide // X
    errs = got[:, :depth]
    own = got[:, depth:]
    lane = lax.broadcasted_iota(jnp.int32, own.shape, 1)
    own32 = own.astype(f32)
    ones_out[...] = jnp.where(lane < feats, own32, 1.0).astype(bf16)
    top_err = jnp.max(jnp.where(lane == feats, own32, 0.0), axis=(0, 1), keepdims=True)
    e_term = exponent(base[:, 0:1] * top_err)
    scale = base[:, 1:2] * jnp.exp2(TOP - e_term)
    for h, w in enumerate((w_own, w_other)):
        term = lax.dot_general(errs, w[...], BY_LAST, preferred_element_type=f32) * scale
        out[:, :chunk, h * lats : (h + 1) * lats] = term.reshape(X, chunk, lats)
    pre = jnp.dot(own, enc_both[...], preferred_element_type=f32) * PRE_SCALE
    out[:, chunk : 2 * chunk, :] = pre.reshape(X, chunk, C * lats)
    row = lax.broadcasted_iota(jnp.int32, lines.shape, 0)
    extra = jnp.where(row == 3, jnp.broadcast_to(e_term, lines.shape), lines[...])
    for i in range(X):
        out[i, 2 * chunk :, :] = extra


def along_x(back, out):
    chunk = (back.shape[1] - EXTRA) // 2
    at = 2 * chunk
    line = lambda i, k: back[i, at + k : at + k + 1, :]
    e_sq, e_term = line(0, 2), line(0, 3)
    for i in range(1, X):
        e_sq, e_term = jnp.maximum(e_sq, line(i, 2)), jnp.maximum(e_term, line(i, 3))
    e_sq, e_term = e_sq + 2.0, e_term + 2.0
    dact, pre, squares = 0.0, 0.0, 0.0
    for i in range(X):
        dact += back[i, :chunk, :] * jnp.exp2(line(i, 3) - e_term)
        pre += back[i, chunk:at, :]
        squares += (line(i, 0) + line(i, 1)) * jnp.exp2(line(i, 2) - e_sq)
    out[:chunk, :] = dact
    out[chunk:at, :] = pre
    hi = squares.astype(bf16).astype(f32)
    out[at : at + 1, :] = hi
    out[at + 1 : at + 2, :] = squares - hi
    out[at + 2 : at + 3, :] = e_sq
    out[at + 3 : at + 4, :] = e_term
    out[at + 4 :, :] = jnp.zeros((EXTRA - 4, out.shape[1]), f32)


def middle(one, two, gates, bias, out):
    chunk = gates.shape[0]
    dact, pre, sumsq = 0.0, 0.0, 0.0
    at = 2 * chunk
    for half in (one, two):
        dact += half[:chunk, :] * jnp.exp2(half[at + 3 : at + 4, :] - TOP)
        pre += half[chunk:at, :]
        squares = half[at : at + 1, :] + half[at + 1 : at + 2, :]
        sumsq += squares * jnp.exp2(half[at + 2 : at + 3, :] - TOP)
    pre = pre * (1.0 / PRE_SCALE) + bias[...]
    norm = jnp.sqrt(sumsq)
    tanh_val = jnp.tanh(sharpness * (gates[...] * pre) * norm)
    grad = gates[...] * (dact + penalty * sharpness * norm * (1.0 - tanh_val * tanh_val))
    grad = grad.astype(bf16)
    for i in range(X):
        out[i] = grad


def backward(feats, grad, enc_both, own_ones, sent, keep, away):
    lats = keep.shape[1]
    part = lax.dot_general(grad[...], enc_both[...], BY_LAST, preferred_element_type=f32)
    e_part = exponent(jnp.max(jnp.abs(part), axis=(0, 1), keepdims=True))
    lane = lax.broadcasted_iota(jnp.int32, part.shape, 1)
    sent[...] = jnp.where(lane < feats, part * jnp.exp2(TOP - e_part), jnp.broadcast_to(e_part, part.shape))
    enc = lax.dot_general(own_ones[...], grad[...], BY_FIRST, preferred_element_type=f32)
    keep[...] = enc[: keep.shape[0], :lats]
    away[...] = enc[: away.shape[0], lats:]


def finish(came, keep, far, grad_in, grad_enc, grad_bias):
    rows, _, feats = grad_in.shape
    values = came[:, :feats] * jnp.exp2(came[:, feats : feats + 1] - TOP)
    values = values.reshape(S, PEERS // S, rows, feats)
    for s in range(S):
        grad_in[:, s, :] = jnp.sum(values[s], axis=0)
    both = keep[...] + far[...]
    grad_enc[...] = both[:feats]
    grad_bias[...] = both[feats : feats + 1]


def local(inputs, w_enc, b_enc, masks, w_dec, errors, target_of):
    yl, core = lax.axis_index("yl"), lax.axis_index("c")
    x = lax.axis_index("x")
    slot = lax.axis_index("yh") * X + x
    source = yl * S // YL
    feats, lats = w_enc.shape
    depth = w_dec.shape[2]
    rows = inputs.shape[0]
    wide = PEERS * rows
    chunk = wide // X
    both_lats = C * lats
    pad = LANES - feats

    held = pl.pallas_call(
        prepare, out_shape=pltpu.HBM((PEERS, rows, depth + LANES), bf16), compiler_params=PARAMS
    )(errors[0], inputs)
    held, masks, w_dec = lax.optimization_barrier((held, masks, w_dec))
    got = lax.all_to_all(held, PLANE, 0, 0, tiled=True).reshape(wide, depth + LANES)

    gates6 = masks.reshape(X, chunk // rows, C, rows, lats)
    gates5 = lax.dynamic_index_in_dim(gates6, x, 0, keepdims=False)
    gates_own = lax.dynamic_index_in_dim(gates5, core, 1, keepdims=False).reshape(chunk, lats)
    gates_send = lax.dynamic_index_in_dim(gates5, 1 - core, 1, keepdims=False).reshape(chunk, lats)
    w_own = w_dec[0]
    square = jnp.einsum("cd,cd->c", w_own, w_own, preferred_element_type=f32)
    w_other = lax.ppermute(w_own, "c", SWAP)
    pack = jnp.concatenate(
        [
            w_enc,
            jnp.zeros((pad, lats), bf16),
            gates_send.astype(bf16),
            split_bf16(b_enc),
            split_bf16(square),
            jnp.zeros((10, lats), bf16),
        ],
        axis=0,
    )
    pack_other = lax.ppermute(pack, "c", SWAP)
    enc_both = jnp.concatenate([pack[:LANES], pack_other[:LANES]], axis=1)
    gates_other = pack_other[LANES : LANES + chunk].astype(f32)
    gates = jnp.concatenate([gates_own.astype(f32), gates_other], axis=1)
    parts = jnp.sum(pack_other[LANES + chunk : LANES + chunk + 6].astype(f32).reshape(2, 3, lats), axis=1)
    b_both = jnp.concatenate([b_enc, parts[0]])[None]

    slots = jnp.arange(target_of.shape[0], dtype=jnp.int32)
    layer = jnp.sum(jnp.where(slots == slot, target_of, 0))
    flag = (layer >= source).astype(f32)
    squares = flag * jnp.concatenate([square, parts[1]])
    top_sq = jnp.max(squares)
    e_sq = exponent(top_sq)
    scaled = squares * jnp.exp2(TOP - e_sq)
    hi = scaled.astype(f16).astype(f32)
    lines = jnp.concatenate(
        [
            hi[None],
            (scaled - hi)[None],
            jnp.broadcast_to(e_sq, (1, both_lats)),
            jnp.zeros((EXTRA - 3, both_lats), f32),
        ],
        axis=0,
    )
    base = jnp.stack([jnp.sqrt(depth * 1.01 * top_sq), flag])[None]
    lines, base, enc_both, gates, b_both, w_other, got = lax.optimization_barrier(
        (lines, base, enc_both, gates, b_both, w_other, got)
    )

    out, own_ones = call(
        functools.partial(forward, feats),
        [((X, 2 * chunk + EXTRA, both_lats), f32), ((wide, LANES), bf16)],
        got, w_own, w_other, enc_both, lines, base,
    )
    back = lax.all_to_all(out.astype(f16), "x", 0, 0, tiled=True).astype(f32)
    (half,) = call(along_x, [((2 * chunk + EXTRA, both_lats), f32)], back)
    half = lax.optimization_barrier(half.astype(f16))
    partner = lax.ppermute(half, "yh", SWAP)
    (grad,) = call(
        middle, [((X, chunk, both_lats), bf16)], half.astype(f32), partner.astype(f32), gates, b_both
    )
    grad = lax.all_to_all(grad, "x", 0, 0, tiled=True).reshape(wide, both_lats)
    sent, keep, away = call(
        functools.partial(backward, feats),
        [((wide, LANES), f32), ((feats + 8, lats), f32), ((feats + 8, lats), f32)],
        grad, enc_both, own_ones,
    )
    far = lax.ppermute(away, "c", SWAP)
    came = lax.all_to_all(sent.astype(f16).reshape(PEERS, rows, LANES), PLANE, 0, 0, tiled=True)
    grad_in, grad_enc, grad_bias = call(
        finish,
        [((rows, S, feats), f32), ((feats, lats), f32), ((1, lats), f32)],
        came.astype(f32).reshape(wide, LANES), keep, far,
    )
    return (grad_enc, grad_bias[0], grad_in)


def solution(mesh):
    fine = Mesh(mesh.devices.reshape(YL, Z, C, YH, X), AXES)
    return jax.shard_map(
        local,
        mesh=fine,
        in_specs=(
            P(LAT, None, TGT),
            P(TGT, LAT),
            P(LAT),
            P(None, LAT),
            P(TGT, LAT, None),
            P(TGT, LAT, None),
            P(),
        ),
        out_specs=(P(TGT, LAT), P(LAT), P(LAT, None, TGT)),
        check_vma=False,
    )
```

```python
import functools

import jax
import jax.numpy as jnp
from jax import lax
from jax.experimental import pallas as pl
from jax.experimental.pallas import tpu as pltpu
from jax.sharding import Mesh, PartitionSpec as P

S = 2
penalty = 1.0
sharpness = 1.0

YL, Z, C, YH, X = 4, 8, 2, 2, 4
AXES = ("yl", "z", "c", "yh", "x")
LAT = ("yl", "z", "c")
TGT = ("yh", "x")
PLANE = ("yl", "z")
PEERS = YL * Z
SLOTS = YH * X
LANES = 384
EXTRA = 8
PRE_SCALE = 64.0
TOP = 14.0
SWAP = [(0, 1), (1, 0)]
f32, bf16, f16 = jnp.float32, jnp.bfloat16, jnp.float16
VMEM = pl.BlockSpec(memory_space=pltpu.VMEM)
BY_LAST = (((1,), (1,)), ((), ()))
BY_FIRST = (((0,), (0,)), ((), ()))
PARAMS = pltpu.CompilerParams(vmem_limit_bytes=24 * 1024 * 1024)


def exponent(bound):
    return jnp.ceil(jnp.log2(jnp.maximum(bound, 1e-30)))


def split_bf16(v):
    hi = v.astype(bf16)
    rest = v - hi.astype(f32)
    mid = rest.astype(bf16)
    low = (rest - mid.astype(f32)).astype(bf16)
    return jnp.stack([hi, mid, low])


def call(body, outs, *args, **kinds):
    shapes = [jax.ShapeDtypeStruct(*o) for o in outs]
    return pl.pallas_call(body, out_shape=shapes, compiler_params=PARAMS, **kinds)(*args)


def prepare(errors_far, inputs_far, out, errors, inputs, arrived):
    fetches = [
        pltpu.make_async_copy(errors_far, errors, arrived.at[0]),
        pltpu.make_async_copy(inputs_far, inputs, arrived.at[1]),
    ]
    for fetch in fetches:
        fetch.start()
    for fetch in fetches:
        fetch.wait()
    rows, depth = errors.shape
    errs = errors[...]
    top_err = jnp.max(jnp.abs(errs.astype(f32)), axis=(0, 1), keepdims=True) * 1.01
    pad = jnp.broadcast_to(top_err, (rows, LANES - inputs.shape[2]))
    for s in range(S):
        last = jnp.concatenate([inputs[:, s, :].astype(f32), pad], axis=1).astype(bf16)
        for i in range(PEERS // S):
            out[s * (PEERS // S) + i, :, :depth] = errs
            out[s * (PEERS // S) + i, :, depth:] = last


def forward(feats, got, w_own, w_far, enc_both, lines, base, out, ones_out, w_other, arrived):
    fetch = pltpu.make_async_copy(w_far, w_other, arrived)
    fetch.start()
    wide = got.shape[0]
    lats, depth = w_own.shape
    chunk = wide // X
    errs = got[:, :depth]
    own = got[:, depth:]
    lane = lax.broadcasted_iota(jnp.int32, own.shape, 1)
    own32 = own.astype(f32)
    ones_out[...] = jnp.where(lane < feats, own32, 1.0).astype(bf16)
    top_err = jnp.max(jnp.where(lane == feats, own32, 0.0), axis=(0, 1), keepdims=True)
    e_term = exponent(base[:, 0:1] * top_err)
    scale = base[:, 1:2] * jnp.exp2(TOP - e_term)
    pre = jnp.dot(own, enc_both[...], preferred_element_type=f32) * PRE_SCALE
    out[:, chunk : 2 * chunk, :] = pre.reshape(X, chunk, C * lats)
    row = lax.broadcasted_iota(jnp.int32, lines.shape, 0)
    extra = jnp.where(row == 3, jnp.broadcast_to(e_term, lines.shape), lines[...])
    for i in range(X):
        out[i, 2 * chunk :, :] = extra
    for h, w in enumerate((w_own, w_other)):
        if h == 1:
            fetch.wait()
        term = lax.dot_general(errs, w[...], BY_LAST, preferred_element_type=f32) * scale
        out[:, :chunk, h * lats : (h + 1) * lats] = term.reshape(X, chunk, lats)


def along_x(back, out):
    chunk = (back.shape[1] - EXTRA) // 2
    at = 2 * chunk
    line = lambda i, k: back[i, at + k : at + k + 1, :]
    e_sq, e_term = line(0, 2), line(0, 3)
    for i in range(1, X):
        e_sq, e_term = jnp.maximum(e_sq, line(i, 2)), jnp.maximum(e_term, line(i, 3))
    e_sq, e_term = e_sq + 2.0, e_term + 2.0
    dact, pre, squares = 0.0, 0.0, 0.0
    for i in range(X):
        dact += back[i, :chunk, :] * jnp.exp2(line(i, 3) - e_term)
        pre += back[i, chunk:at, :]
        squares += (line(i, 0) + line(i, 1)) * jnp.exp2(line(i, 2) - e_sq)
    out[:chunk, :] = dact
    out[chunk:at, :] = pre
    hi = squares.astype(bf16).astype(f32)
    out[at : at + 1, :] = hi
    out[at + 1 : at + 2, :] = squares - hi
    out[at + 2 : at + 3, :] = e_sq
    out[at + 3 : at + 4, :] = e_term
    out[at + 4 :, :] = jnp.zeros((EXTRA - 4, out.shape[1]), f32)


def middle(one, two, gates, bias, out):
    chunk = gates.shape[0]
    dact, pre, sumsq = 0.0, 0.0, 0.0
    at = 2 * chunk
    for half in (one, two):
        dact += half[:chunk, :] * jnp.exp2(half[at + 3 : at + 4, :] - TOP)
        pre += half[chunk:at, :]
        squares = half[at : at + 1, :] + half[at + 1 : at + 2, :]
        sumsq += squares * jnp.exp2(half[at + 2 : at + 3, :] - TOP)
    pre = pre * (1.0 / PRE_SCALE) + bias[...]
    norm = jnp.sqrt(sumsq)
    tanh_val = jnp.tanh(sharpness * (gates[...] * pre) * norm)
    grad = gates[...] * (dact + penalty * sharpness * norm * (1.0 - tanh_val * tanh_val))
    grad = grad.astype(bf16)
    for i in range(X):
        out[i] = grad


def backward(feats, grad, enc_both, own_ones, sent, keep, away):
    lats = keep.shape[1]
    part = lax.dot_general(grad[...], enc_both[...], BY_LAST, preferred_element_type=f32)
    e_part = exponent(jnp.max(jnp.abs(part), axis=(0, 1), keepdims=True))
    lane = lax.broadcasted_iota(jnp.int32, part.shape, 1)
    sent[...] = jnp.where(lane < feats, part * jnp.exp2(TOP - e_part), jnp.broadcast_to(e_part, part.shape))
    enc = lax.dot_general(own_ones[...], grad[...], BY_FIRST, preferred_element_type=f32)
    keep[...] = enc[: keep.shape[0], :lats]
    away[...] = enc[: away.shape[0], lats:]


def finish(came, keep, far, grad_in, grad_enc, grad_bias):
    rows, _, feats = grad_in.shape
    values = came[:, :feats] * jnp.exp2(came[:, feats : feats + 1] - TOP)
    values = values.reshape(S, PEERS // S, rows, feats)
    for s in range(S):
        grad_in[:, s, :] = jnp.sum(values[s], axis=0)
    both = keep[...] + far[...]
    grad_enc[...] = both[:feats]
    grad_bias[...] = both[feats : feats + 1]


def local(inputs, w_enc, b_enc, masks, w_dec, errors, target_of):
    yl, core = lax.axis_index("yl"), lax.axis_index("c")
    x = lax.axis_index("x")
    slot = lax.axis_index("yh") * X + x
    source = yl * S // YL
    feats, lats = w_enc.shape
    depth = w_dec.shape[2]
    rows = inputs.shape[0]
    wide = PEERS * rows
    chunk = wide // X
    both_lats = C * lats
    pad = LANES - feats

    held = pl.pallas_call(
        prepare,
        out_shape=pltpu.HBM((PEERS, rows, depth + LANES), bf16),
        in_specs=[pl.BlockSpec(memory_space=pltpu.HBM)] * 2,
        scratch_shapes=[
            pltpu.VMEM(errors.shape[1:], bf16),
            pltpu.VMEM(inputs.shape, bf16),
            pltpu.SemaphoreType.DMA((2,)),
        ],
        compiler_params=PARAMS,
    )(*(pltpu.with_memory_space_constraint(v, pltpu.HBM) for v in (errors[0], inputs)))
    held, masks, w_dec = lax.optimization_barrier((held, masks, w_dec))
    got = lax.all_to_all(held, PLANE, 0, 0, tiled=True).reshape(wide, depth + LANES)

    gates6 = masks.reshape(X, chunk // rows, C, rows, lats)
    gates5 = lax.dynamic_index_in_dim(gates6, x, 0, keepdims=False)
    gates_own = lax.dynamic_index_in_dim(gates5, core, 1, keepdims=False).reshape(chunk, lats)
    gates_send = lax.dynamic_index_in_dim(gates5, 1 - core, 1, keepdims=False).reshape(chunk, lats)
    w_own = w_dec[0]
    square = jnp.einsum("cd,cd->c", w_own, w_own, preferred_element_type=f32)
    w_other = lax.ppermute(w_own, "c", SWAP)
    pack = jnp.concatenate(
        [
            w_enc,
            jnp.zeros((pad, lats), bf16),
            gates_send.astype(bf16),
            split_bf16(b_enc),
            split_bf16(square),
            jnp.zeros((10, lats), bf16),
        ],
        axis=0,
    )
    pack_other = lax.ppermute(pack, "c", SWAP)
    enc_both = jnp.concatenate([pack[:LANES], pack_other[:LANES]], axis=1)
    gates_other = pack_other[LANES : LANES + chunk].astype(f32)
    gates = jnp.concatenate([gates_own.astype(f32), gates_other], axis=1)
    parts = jnp.sum(pack_other[LANES + chunk : LANES + chunk + 6].astype(f32).reshape(2, 3, lats), axis=1)
    b_both = jnp.concatenate([b_enc, parts[0]])[None]

    slots = jnp.arange(target_of.shape[0], dtype=jnp.int32)
    layer = jnp.sum(jnp.where(slots == slot, target_of, 0))
    flag = (layer >= source).astype(f32)
    squares = flag * jnp.concatenate([square, parts[1]])
    top_sq = jnp.max(squares)
    e_sq = exponent(top_sq)
    scaled = squares * jnp.exp2(TOP - e_sq)
    hi = scaled.astype(f16).astype(f32)
    lines = jnp.concatenate(
        [
            hi[None],
            (scaled - hi)[None],
            jnp.broadcast_to(e_sq, (1, both_lats)),
            jnp.zeros((EXTRA - 3, both_lats), f32),
        ],
        axis=0,
    )
    base = jnp.stack([jnp.sqrt(depth * 1.01 * top_sq), flag])[None]
    lines, base, enc_both, gates, b_both, w_other, got = lax.optimization_barrier(
        (lines, base, enc_both, gates, b_both, w_other, got)
    )

    out, own_ones = call(
        functools.partial(forward, feats),
        [((X, 2 * chunk + EXTRA, both_lats), f32), ((wide, LANES), bf16)],
        got, w_own, w_other, enc_both, lines, base,
        in_specs=[VMEM, VMEM, pl.BlockSpec(memory_space=pl.ANY), VMEM, VMEM, VMEM],
        scratch_shapes=[pltpu.VMEM((lats, depth), bf16), pltpu.SemaphoreType.DMA],
    )
    back = lax.all_to_all(out.astype(f16), "x", 0, 0, tiled=True).astype(f32)
    (half,) = call(along_x, [((2 * chunk + EXTRA, both_lats), f32)], back)
    half = lax.optimization_barrier(half.astype(f16))
    partner = lax.ppermute(half, "yh", SWAP)
    (grad,) = call(
        middle, [((X, chunk, both_lats), bf16)], half.astype(f32), partner.astype(f32), gates, b_both
    )
    grad = lax.all_to_all(grad, "x", 0, 0, tiled=True).reshape(wide, both_lats)
    sent, keep, away = call(
        functools.partial(backward, feats),
        [((wide, LANES), f32), ((feats + 8, lats), f32), ((feats + 8, lats), f32)],
        grad, enc_both, own_ones,
    )
    far = lax.ppermute(away, "c", SWAP)
    came = lax.all_to_all(sent.astype(f16).reshape(PEERS, rows, LANES), PLANE, 0, 0, tiled=True)
    grad_in, grad_enc, grad_bias = call(
        finish,
        [((rows, S, feats), f32), ((feats, lats), f32), ((1, lats), f32)],
        came.astype(f32).reshape(wide, LANES), keep, far,
    )
    return (grad_enc, grad_bias[0], grad_in)


def solution(mesh):
    fine = Mesh(mesh.devices.reshape(YL, Z, C, YH, X), AXES)
    return jax.shard_map(
        local,
        mesh=fine,
        in_specs=(
            P(LAT, None, TGT),
            P(TGT, LAT),
            P(LAT),
            P(None, LAT),
            P(TGT, LAT, None),
            P(TGT, LAT, None),
            P(),
        ),
        out_specs=(P(TGT, LAT), P(LAT), P(LAT, None, TGT)),
        check_vma=False,
    )
```

```python
import functools

import jax
import jax.numpy as jnp
from jax import lax
from jax.experimental import pallas as pl
from jax.experimental.pallas import tpu as pltpu
from jax.sharding import Mesh, PartitionSpec as P

S = 2
penalty = 1.0
sharpness = 1.0

YL, Z, C, YH, X = 4, 8, 2, 2, 4
AXES = ("yl", "z", "c", "yh", "x")
LAT = ("yl", "z", "c")
TGT = ("yh", "x")
PLANE = ("yl", "z")
PEERS = YL * Z
SLOTS = YH * X
LANES = 384
EXTRA = 8
PRE_SCALE = 64.0
TOP = 14.0
SWAP = [(0, 1), (1, 0)]
f32, bf16, f16 = jnp.float32, jnp.bfloat16, jnp.float16
BY_LAST = (((1,), (1,)), ((), ()))
BY_FIRST = (((0,), (0,)), ((), ()))
PARAMS = pltpu.CompilerParams(vmem_limit_bytes=24 * 1024 * 1024)


def exponent(bound):
    return jnp.ceil(jnp.log2(jnp.maximum(bound, 1e-30)))


def split_bf16(v):
    hi = v.astype(bf16)
    rest = v - hi.astype(f32)
    mid = rest.astype(bf16)
    low = (rest - mid.astype(f32)).astype(bf16)
    return jnp.stack([hi, mid, low])


def call(body, outs, *args):
    shapes = [jax.ShapeDtypeStruct(*o) for o in outs]
    return pl.pallas_call(body, out_shape=shapes, compiler_params=PARAMS)(*args)


def prepare(errors_far, inputs_far, out, errors, inputs, arrived):
    fetches = [
        pltpu.make_async_copy(errors_far, errors, arrived.at[0]),
        pltpu.make_async_copy(inputs_far, inputs, arrived.at[1]),
    ]
    for fetch in fetches:
        fetch.start()
    for fetch in fetches:
        fetch.wait()
    rows, depth = errors.shape
    errs = errors[...]
    top_err = jnp.max(jnp.abs(errs.astype(f32)), axis=(0, 1), keepdims=True) * 1.01
    pad = jnp.broadcast_to(top_err, (rows, LANES - inputs.shape[2]))
    for s in range(S):
        last = jnp.concatenate([inputs[:, s, :].astype(f32), pad], axis=1).astype(bf16)
        for i in range(PEERS // S):
            out[s * (PEERS // S) + i, :, :depth] = errs
            out[s * (PEERS // S) + i, :, depth:] = last


def first(feats, last, enc_both, lines, base, out, ones_out, tops):
    wide = last.shape[0]
    chunk = wide // X
    own = last[...]
    lane = lax.broadcasted_iota(jnp.int32, own.shape, 1)
    own32 = own.astype(f32)
    ones_out[...] = jnp.where(lane < feats, own32, 1.0).astype(bf16)
    top_err = jnp.max(jnp.where(lane == feats, own32, 0.0), axis=(0, 1), keepdims=True)
    e_term = exponent(base[:, 0:1] * top_err)
    tops[...] = jnp.broadcast_to(e_term, tops.shape)
    pre = jnp.dot(own, enc_both[...], preferred_element_type=f32) * PRE_SCALE
    out[:, :chunk, :] = pre.reshape(X, chunk, enc_both.shape[1])
    row = lax.broadcasted_iota(jnp.int32, lines.shape, 0)
    extra = jnp.where(row == 3, jnp.broadcast_to(e_term, lines.shape), lines[...])
    for i in range(X):
        out[i, chunk:, :] = extra


def terms(errs, w_own, w_far, tops, base, out, w_other, arrived):
    fetch = pltpu.make_async_copy(w_far, w_other, arrived)
    fetch.start()
    lats = w_own.shape[0]
    chunk = errs.shape[0] // X
    scale = base[:, 1:2] * jnp.exp2(TOP - tops[0:1, 0:1])
    for h, w in enumerate((w_own, w_other)):
        if h == 1:
            fetch.wait()
        term = lax.dot_general(errs[...], w[...], BY_LAST, preferred_element_type=f32) * scale
        out[:, :, h * lats : (h + 1) * lats] = term.reshape(X, chunk, lats)


def pre_along_x(back, out, weights):
    at = back.shape[1] - EXTRA
    line = lambda i, k: back[i, at + k : at + k + 1, :]
    e_sq, e_term = line(0, 2), line(0, 3)
    for i in range(1, X):
        e_sq, e_term = jnp.maximum(e_sq, line(i, 2)), jnp.maximum(e_term, line(i, 3))
    e_sq, e_term = e_sq + 2.0, e_term + 2.0
    pre, squares = 0.0, 0.0
    for i in range(X):
        pre += back[i, :at, :]
        squares += (line(i, 0) + line(i, 1)) * jnp.exp2(line(i, 2) - e_sq)
        weights[i : i + 1, :] = jnp.exp2(line(i, 3) - e_term)
    weights[X:, :] = jnp.zeros((EXTRA - X, out.shape[1]), f32)
    out[:at, :] = pre
    hi = squares.astype(bf16).astype(f32)
    out[at : at + 1, :] = hi
    out[at + 1 : at + 2, :] = squares - hi
    out[at + 2 : at + 3, :] = e_sq
    out[at + 3 : at + 4, :] = e_term
    out[at + 4 :, :] = jnp.zeros((EXTRA - 4, out.shape[1]), f32)


def terms_along_x(back, weights, out):
    total = 0.0
    for i in range(X):
        total += back[i] * weights[i : i + 1, :]
    out[...] = total


def penalties(one, two, gates, bias, out, weights):
    at = gates.shape[0]
    pre, sumsq = 0.0, 0.0
    for k, half in enumerate((one, two)):
        pre += half[:at, :]
        squares = half[at : at + 1, :] + half[at + 1 : at + 2, :]
        sumsq += squares * jnp.exp2(half[at + 2 : at + 3, :] - TOP)
        weights[k : k + 1, :] = jnp.exp2(half[at + 3 : at + 4, :] - TOP)
    weights[2:, :] = jnp.zeros((EXTRA - 2, gates.shape[1]), f32)
    pre = pre * (1.0 / PRE_SCALE) + bias[...]
    norm = jnp.sqrt(sumsq)
    tanh_val = jnp.tanh(sharpness * (gates[...] * pre) * norm)
    out[...] = penalty * sharpness * norm * (1.0 - tanh_val * tanh_val)


def gradient(one, two, weights, pull, gates, out):
    dact = one[...] * weights[0:1, :] + two[...] * weights[1:2, :]
    grad = (gates[...] * (dact + pull[...])).astype(bf16)
    for i in range(X):
        out[i] = grad


def backward(feats, grad, enc_both, own_ones, sent, keep, away):
    lats = keep.shape[1]
    part = lax.dot_general(grad[...], enc_both[...], BY_LAST, preferred_element_type=f32)
    e_part = exponent(jnp.max(jnp.abs(part), axis=(0, 1), keepdims=True))
    lane = lax.broadcasted_iota(jnp.int32, part.shape, 1)
    sent[...] = jnp.where(lane < feats, part * jnp.exp2(TOP - e_part), jnp.broadcast_to(e_part, part.shape))
    enc = lax.dot_general(own_ones[...], grad[...], BY_FIRST, preferred_element_type=f32)
    keep[...] = enc[: keep.shape[0], :lats]
    away[...] = enc[: away.shape[0], lats:]


def finish(came, keep, far, grad_in, grad_enc, grad_bias):
    rows, _, feats = grad_in.shape
    values = came[:, :feats] * jnp.exp2(came[:, feats : feats + 1] - TOP)
    values = values.reshape(S, PEERS // S, rows, feats)
    for s in range(S):
        grad_in[:, s, :] = jnp.sum(values[s], axis=0)
    both = keep[...] + far[...]
    grad_enc[...] = both[:feats]
    grad_bias[...] = both[feats : feats + 1]


def local(inputs, w_enc, b_enc, masks, w_dec, errors, target_of):
    yl, core = lax.axis_index("yl"), lax.axis_index("c")
    x = lax.axis_index("x")
    slot = lax.axis_index("yh") * X + x
    source = yl * S // YL
    feats, lats = w_enc.shape
    depth = w_dec.shape[2]
    rows = inputs.shape[0]
    wide = PEERS * rows
    chunk = wide // X
    both_lats = C * lats
    pad = LANES - feats

    held = pl.pallas_call(
        prepare,
        out_shape=pltpu.HBM((PEERS, rows, depth + LANES), bf16),
        in_specs=[pl.BlockSpec(memory_space=pltpu.HBM)] * 2,
        scratch_shapes=[
            pltpu.VMEM(errors.shape[1:], bf16),
            pltpu.VMEM(inputs.shape, bf16),
            pltpu.SemaphoreType.DMA((2,)),
        ],
        compiler_params=PARAMS,
    )(*(pltpu.with_memory_space_constraint(v, pltpu.HBM) for v in (errors[0], inputs)))
    held, masks, w_dec = lax.optimization_barrier((held, masks, w_dec))
    got = lax.all_to_all(held, PLANE, 0, 0, tiled=True).reshape(wide, depth + LANES)

    gates6 = masks.reshape(X, chunk // rows, C, rows, lats)
    gates5 = lax.dynamic_index_in_dim(gates6, x, 0, keepdims=False)
    gates_own = lax.dynamic_index_in_dim(gates5, core, 1, keepdims=False).reshape(chunk, lats)
    gates_send = lax.dynamic_index_in_dim(gates5, 1 - core, 1, keepdims=False).reshape(chunk, lats)
    w_own = w_dec[0]
    square = jnp.einsum("cd,cd->c", w_own, w_own, preferred_element_type=f32)
    w_other = lax.ppermute(w_own, "c", SWAP)
    pack = jnp.concatenate(
        [
            w_enc,
            jnp.zeros((pad, lats), bf16),
            gates_send.astype(bf16),
            split_bf16(b_enc),
            split_bf16(square),
            jnp.zeros((10, lats), bf16),
        ],
        axis=0,
    )
    pack_other = lax.ppermute(pack, "c", SWAP)
    enc_both = jnp.concatenate([pack[:LANES], pack_other[:LANES]], axis=1)
    gates_other = pack_other[LANES : LANES + chunk].astype(f32)
    gates = jnp.concatenate([gates_own.astype(f32), gates_other], axis=1)
    parts = jnp.sum(pack_other[LANES + chunk : LANES + chunk + 6].astype(f32).reshape(2, 3, lats), axis=1)
    b_both = jnp.concatenate([b_enc, parts[0]])[None]

    slots = jnp.arange(target_of.shape[0], dtype=jnp.int32)
    layer = jnp.sum(jnp.where(slots == slot, target_of, 0))
    flag = (layer >= source).astype(f32)
    squares = flag * jnp.concatenate([square, parts[1]])
    top_sq = jnp.max(squares)
    e_sq = exponent(top_sq)
    scaled = squares * jnp.exp2(TOP - e_sq)
    hi = scaled.astype(f16).astype(f32)
    lines = jnp.concatenate(
        [
            hi[None],
            (scaled - hi)[None],
            jnp.broadcast_to(e_sq, (1, both_lats)),
            jnp.zeros((EXTRA - 3, both_lats), f32),
        ],
        axis=0,
    )
    base = jnp.stack([jnp.sqrt(depth * 1.01 * top_sq), flag])[None]
    lines, base, enc_both, gates, b_both, w_other, got = lax.optimization_barrier(
        (lines, base, enc_both, gates, b_both, w_other, got)
    )

    whole = lambda shape: pl.BlockSpec(shape, lambda i: (0,) * len(shape))
    pre_out, own_ones, tops = pl.pallas_call(
        functools.partial(first, feats),
        grid=(1,),
        in_specs=[
            pl.BlockSpec((wide, LANES), lambda i: (0, depth // LANES)),
            whole((LANES, both_lats)),
            whole((EXTRA, both_lats)),
            whole((1, 2)),
        ],
        out_specs=[whole((X, chunk + EXTRA, both_lats)), whole((wide, LANES)), whole((EXTRA, 128))],
        out_shape=[
            jax.ShapeDtypeStruct((X, chunk + EXTRA, both_lats), f32),
            jax.ShapeDtypeStruct((wide, LANES), bf16),
            jax.ShapeDtypeStruct((EXTRA, 128), f32),
        ],
        compiler_params=PARAMS,
    )(got, enc_both, lines, base)
    pre_in = lax.all_to_all(pre_out.astype(f16), "x", 0, 0, tiled=True).astype(f32)
    term = pl.pallas_call(
        terms,
        grid=(1,),
        in_specs=[
            whole((wide, depth)),
            whole((lats, depth)),
            pl.BlockSpec(memory_space=pl.ANY),
            whole((EXTRA, 128)),
            whole((1, 2)),
        ],
        out_specs=whole((X, chunk, both_lats)),
        out_shape=jax.ShapeDtypeStruct((X, chunk, both_lats), f32),
        scratch_shapes=[pltpu.VMEM((lats, depth), bf16), pltpu.SemaphoreType.DMA],
        compiler_params=PARAMS,
        cost_estimate=pl.CostEstimate(
            flops=2 * wide * depth * both_lats,
            bytes_accessed=2 * (wide + both_lats) * depth + 4 * wide * both_lats,
            transcendentals=0,
        ),
    )(got, w_own, w_other, tops, base)
    terms_in = lax.all_to_all(term.astype(f16), "x", 0, 0, tiled=True).astype(f32)

    half, weights = call(
        pre_along_x, [((chunk + EXTRA, both_lats), f32), ((EXTRA, both_lats), f32)], pre_in
    )
    half = lax.optimization_barrier(half.astype(f16))
    partner = lax.ppermute(half, "yh", SWAP)
    (term_half,) = call(terms_along_x, [((chunk, both_lats), f32)], terms_in, weights)
    term_half = lax.optimization_barrier(term_half.astype(f16))
    term_partner = lax.ppermute(term_half, "yh", SWAP)
    pull, weights = call(
        penalties,
        [((chunk, both_lats), f32), ((EXTRA, both_lats), f32)],
        half.astype(f32), partner.astype(f32), gates, b_both,
    )
    (grad,) = call(
        gradient,
        [((X, chunk, both_lats), bf16)],
        term_half.astype(f32), term_partner.astype(f32), weights, pull, gates,
    )
    grad = lax.all_to_all(grad, "x", 0, 0, tiled=True).reshape(wide, both_lats)
    sent, keep, away = call(
        functools.partial(backward, feats),
        [((wide, LANES), f32), ((feats + 8, lats), f32), ((feats + 8, lats), f32)],
        grad, enc_both, own_ones,
    )
    far = lax.ppermute(away, "c", SWAP)
    came = lax.all_to_all(sent.astype(f16).reshape(PEERS, rows, LANES), PLANE, 0, 0, tiled=True)
    grad_in, grad_enc, grad_bias = call(
        finish,
        [((rows, S, feats), f32), ((feats, lats), f32), ((1, lats), f32)],
        came.astype(f32).reshape(wide, LANES), keep, far,
    )
    return (grad_enc, grad_bias[0], grad_in)


def solution(mesh):
    fine = Mesh(mesh.devices.reshape(YL, Z, C, YH, X), AXES)
    return jax.shard_map(
        local,
        mesh=fine,
        in_specs=(
            P(LAT, None, TGT),
            P(TGT, LAT),
            P(LAT),
            P(None, LAT),
            P(TGT, LAT, None),
            P(TGT, LAT, None),
            P(),
        ),
        out_specs=(P(TGT, LAT), P(LAT), P(LAT, None, TGT)),
        check_vma=False,
    )
```

```python
import functools

import jax
import jax.numpy as jnp
from jax import lax
from jax.experimental import pallas as pl
from jax.experimental.pallas import tpu as pltpu
from jax.sharding import Mesh, PartitionSpec as P

S = 2
penalty = 1.0
sharpness = 1.0

YL, Z, C, YH, X = 4, 8, 2, 2, 4
AXES = ("yl", "z", "c", "yh", "x")
LAT = ("yl", "z", "c")
TGT = ("yh", "x")
PLANE = ("yl", "z")
PEERS = YL * Z
SLOTS = YH * X
LANES = 384
EXTRA = 8
PRE_SCALE = 64.0
TOP = 14.0
SWAP = [(0, 1), (1, 0)]
f32, bf16, f16 = jnp.float32, jnp.bfloat16, jnp.float16
BY_LAST = (((1,), (1,)), ((), ()))
BY_FIRST = (((0,), (0,)), ((), ()))
PARAMS = pltpu.CompilerParams(vmem_limit_bytes=24 * 1024 * 1024)


def exponent(bound):
    return jnp.ceil(jnp.log2(jnp.maximum(bound, 1e-30)))


def split_bf16(v):
    hi = v.astype(bf16)
    rest = v - hi.astype(f32)
    mid = rest.astype(bf16)
    low = (rest - mid.astype(f32)).astype(bf16)
    return jnp.stack([hi, mid, low])


def call(body, outs, *args):
    shapes = [jax.ShapeDtypeStruct(*o) for o in outs]
    return pl.pallas_call(body, out_shape=shapes, compiler_params=PARAMS)(*args)


def prepare(errors_far, inputs_far, out, errors, inputs, arrived):
    fetches = [
        pltpu.make_async_copy(errors_far, errors, arrived.at[0]),
        pltpu.make_async_copy(inputs_far, inputs, arrived.at[1]),
    ]
    for fetch in fetches:
        fetch.start()
    for fetch in fetches:
        fetch.wait()
    rows, depth = errors.shape
    errs = errors[...]
    top_err = jnp.max(jnp.abs(errs.astype(f32)), axis=(0, 1), keepdims=True) * 1.01
    pad = jnp.broadcast_to(top_err, (rows, LANES - inputs.shape[2]))
    for s in range(S):
        last = jnp.concatenate([inputs[:, s, :].astype(f32), pad], axis=1).astype(bf16)
        for i in range(PEERS // S):
            out[s * (PEERS // S) + i, :, :depth] = errs
            out[s * (PEERS // S) + i, :, depth:] = last


def first(feats, last, enc_both, lines, base, out, ones_out, tops):
    wide = last.shape[0]
    chunk = wide // X
    own = last[...]
    lane = lax.broadcasted_iota(jnp.int32, own.shape, 1)
    own32 = own.astype(f32)
    ones_out[...] = jnp.where(lane < feats, own32, 1.0).astype(bf16)
    top_err = jnp.max(jnp.where(lane == feats, own32, 0.0), axis=(0, 1), keepdims=True)
    e_term = exponent(base[:, 0:1] * top_err)
    tops[...] = jnp.broadcast_to(e_term, tops.shape)
    pre = jnp.dot(own, enc_both[...], preferred_element_type=f32) * PRE_SCALE
    out[:, :chunk, :] = pre.reshape(X, chunk, enc_both.shape[1])
    row = lax.broadcasted_iota(jnp.int32, lines.shape, 0)
    extra = jnp.where(row == 3, jnp.broadcast_to(e_term, lines.shape), lines[...])
    for i in range(X):
        out[i, chunk:, :] = extra


def terms(errs, w_own, w_far, tops, base, out, w_other, arrived):
    fetch = pltpu.make_async_copy(w_far, w_other, arrived)
    fetch.start()
    lats = w_own.shape[0]
    chunk = errs.shape[0] // X
    scale = base[:, 1:2] * jnp.exp2(TOP - tops[0:1, 0:1])
    for h, w in enumerate((w_own, w_other)):
        if h == 1:
            fetch.wait()
        term = lax.dot_general(errs[...], w[...], BY_LAST, preferred_element_type=f32) * scale
        out[:, :, h * lats : (h + 1) * lats] = term.reshape(X, chunk, lats)


def pre_along_x(back, out, weights):
    at = back.shape[1] - EXTRA
    line = lambda i, k: back[i, at + k : at + k + 1, :]
    e_sq, e_term = line(0, 2), line(0, 3)
    for i in range(1, X):
        e_sq, e_term = jnp.maximum(e_sq, line(i, 2)), jnp.maximum(e_term, line(i, 3))
    e_sq, e_term = e_sq + 2.0, e_term + 2.0
    pre, squares = 0.0, 0.0
    for i in range(X):
        pre += back[i, :at, :]
        squares += (line(i, 0) + line(i, 1)) * jnp.exp2(line(i, 2) - e_sq)
        weights[i : i + 1, :] = jnp.exp2(line(i, 3) - e_term)
    weights[X:, :] = jnp.zeros((EXTRA - X, out.shape[1]), f32)
    out[:at, :] = pre
    hi = squares.astype(bf16).astype(f32)
    out[at : at + 1, :] = hi
    out[at + 1 : at + 2, :] = squares - hi
    out[at + 2 : at + 3, :] = e_sq
    out[at + 3 : at + 4, :] = e_term
    out[at + 4 :, :] = jnp.zeros((EXTRA - 4, out.shape[1]), f32)


def terms_along_x(back, weights, out):
    total = 0.0
    for i in range(X):
        total += back[i] * weights[i : i + 1, :]
    out[...] = total


def penalties(one, two, gates, bias, out, weights):
    at = gates.shape[0]
    pre, sumsq = 0.0, 0.0
    for k, half in enumerate((one, two)):
        pre += half[:at, :]
        squares = half[at : at + 1, :] + half[at + 1 : at + 2, :]
        sumsq += squares * jnp.exp2(half[at + 2 : at + 3, :] - TOP)
        weights[k : k + 1, :] = jnp.exp2(half[at + 3 : at + 4, :] - TOP)
    weights[2:, :] = jnp.zeros((EXTRA - 2, gates.shape[1]), f32)
    pre = pre * (1.0 / PRE_SCALE) + bias[...]
    norm = jnp.sqrt(sumsq)
    tanh_val = jnp.tanh(sharpness * (gates[...] * pre) * norm)
    out[...] = penalty * sharpness * norm * (1.0 - tanh_val * tanh_val)


def gradient(one, two, weights, pull, gates, out):
    dact = one[...] * weights[0:1, :] + two[...] * weights[1:2, :]
    grad = (gates[...] * (dact + pull[...])).astype(bf16)
    for i in range(X):
        out[i] = grad


def backward(feats, grad, enc_both, own_ones, sent, keep, away):
    lats = keep.shape[1]
    part = lax.dot_general(grad[...], enc_both[...], BY_LAST, preferred_element_type=f32)
    e_part = exponent(jnp.max(jnp.abs(part), axis=(0, 1), keepdims=True))
    lane = lax.broadcasted_iota(jnp.int32, part.shape, 1)
    sent[...] = jnp.where(lane < feats, part * jnp.exp2(TOP - e_part), jnp.broadcast_to(e_part, part.shape))
    enc = lax.dot_general(own_ones[...], grad[...], BY_FIRST, preferred_element_type=f32)
    keep[...] = enc[: keep.shape[0], :lats]
    away[...] = enc[: away.shape[0], lats:]


def finish(came, keep, far, grad_in, grad_enc, grad_bias):
    rows, _, feats = grad_in.shape
    values = came[:, :feats] * jnp.exp2(came[:, feats : feats + 1] - TOP)
    values = values.reshape(S, PEERS // S, rows, feats)
    for s in range(S):
        grad_in[:, s, :] = jnp.sum(values[s], axis=0)
    both = keep[...] + far[...]
    grad_enc[...] = both[:feats]
    grad_bias[...] = both[feats : feats + 1]


def local(inputs, w_enc, b_enc, masks, w_dec, errors, target_of):
    yl, core = lax.axis_index("yl"), lax.axis_index("c")
    x = lax.axis_index("x")
    slot = lax.axis_index("yh") * X + x
    source = yl * S // YL
    feats, lats = w_enc.shape
    depth = w_dec.shape[2]
    rows = inputs.shape[0]
    wide = PEERS * rows
    chunk = wide // X
    both_lats = C * lats
    pad = LANES - feats

    held = pl.pallas_call(
        prepare,
        out_shape=pltpu.HBM((PEERS, rows, depth + LANES), bf16),
        in_specs=[pl.BlockSpec(memory_space=pltpu.HBM)] * 2,
        scratch_shapes=[
            pltpu.VMEM(errors.shape[1:], bf16),
            pltpu.VMEM(inputs.shape, bf16),
            pltpu.SemaphoreType.DMA((2,)),
        ],
        compiler_params=PARAMS,
    )(*(pltpu.with_memory_space_constraint(v, pltpu.HBM) for v in (errors[0], inputs)))
    held, masks, w_dec = lax.optimization_barrier((held, masks, w_dec))
    got = lax.all_to_all(held, PLANE, 0, 0, tiled=True).reshape(wide, depth + LANES)

    gates6 = masks.reshape(X, chunk // rows, C, rows, lats)
    gates5 = lax.dynamic_index_in_dim(gates6, x, 0, keepdims=False)
    gates_own = lax.dynamic_index_in_dim(gates5, core, 1, keepdims=False).reshape(chunk, lats)
    gates_send = lax.dynamic_index_in_dim(gates5, 1 - core, 1, keepdims=False).reshape(chunk, lats)
    w_own = w_dec[0]
    square = jnp.einsum("cd,cd->c", w_own, w_own, preferred_element_type=f32)
    pack = jnp.concatenate(
        [
            w_enc,
            jnp.zeros((pad, lats), bf16),
            gates_send.astype(bf16),
            split_bf16(b_enc),
            split_bf16(square),
            jnp.zeros((10, lats), bf16),
        ],
        axis=0,
    )
    pack_other = lax.ppermute(pack, "c", SWAP)
    w_late, pack_other = lax.optimization_barrier((w_own, pack_other))
    w_other = lax.ppermute(w_late, "c", SWAP)
    enc_both = jnp.concatenate([pack[:LANES], pack_other[:LANES]], axis=1)
    gates_other = pack_other[LANES : LANES + chunk].astype(f32)
    gates = jnp.concatenate([gates_own.astype(f32), gates_other], axis=1)
    parts = jnp.sum(pack_other[LANES + chunk : LANES + chunk + 6].astype(f32).reshape(2, 3, lats), axis=1)
    b_both = jnp.concatenate([b_enc, parts[0]])[None]

    slots = jnp.arange(target_of.shape[0], dtype=jnp.int32)
    layer = jnp.sum(jnp.where(slots == slot, target_of, 0))
    flag = (layer >= source).astype(f32)
    squares = flag * jnp.concatenate([square, parts[1]])
    top_sq = jnp.max(squares)
    e_sq = exponent(top_sq)
    scaled = squares * jnp.exp2(TOP - e_sq)
    hi = scaled.astype(f16).astype(f32)
    lines = jnp.concatenate(
        [
            hi[None],
            (scaled - hi)[None],
            jnp.broadcast_to(e_sq, (1, both_lats)),
            jnp.zeros((EXTRA - 3, both_lats), f32),
        ],
        axis=0,
    )
    base = jnp.stack([jnp.sqrt(depth * 1.01 * top_sq), flag])[None]
    lines, base, enc_both, gates, b_both, got = lax.optimization_barrier(
        (lines, base, enc_both, gates, b_both, got)
    )

    whole = lambda shape: pl.BlockSpec(shape, lambda i: (0,) * len(shape))
    pre_out, own_ones, tops = pl.pallas_call(
        functools.partial(first, feats),
        grid=(1,),
        in_specs=[
            pl.BlockSpec((wide, LANES), lambda i: (0, depth // LANES)),
            whole((LANES, both_lats)),
            whole((EXTRA, both_lats)),
            whole((1, 2)),
        ],
        out_specs=[whole((X, chunk + EXTRA, both_lats)), whole((wide, LANES)), whole((EXTRA, 128))],
        out_shape=[
            jax.ShapeDtypeStruct((X, chunk + EXTRA, both_lats), f32),
            jax.ShapeDtypeStruct((wide, LANES), bf16),
            jax.ShapeDtypeStruct((EXTRA, 128), f32),
        ],
        compiler_params=PARAMS,
    )(got, enc_both, lines, base)
    pre_in = lax.all_to_all(pre_out.astype(f16), "x", 0, 0, tiled=True).astype(f32)
    term = pl.pallas_call(
        terms,
        grid=(1,),
        in_specs=[
            whole((wide, depth)),
            whole((lats, depth)),
            pl.BlockSpec(memory_space=pl.ANY),
            whole((EXTRA, 128)),
            whole((1, 2)),
        ],
        out_specs=whole((X, chunk, both_lats)),
        out_shape=jax.ShapeDtypeStruct((X, chunk, both_lats), f32),
        scratch_shapes=[pltpu.VMEM((lats, depth), bf16), pltpu.SemaphoreType.DMA],
        compiler_params=PARAMS,
        cost_estimate=pl.CostEstimate(
            flops=2 * wide * depth * both_lats,
            bytes_accessed=2 * (wide + both_lats) * depth + 4 * wide * both_lats,
            transcendentals=0,
        ),
    )(got, w_own, w_other, tops, base)
    terms_in = lax.all_to_all(term.astype(f16), "x", 0, 0, tiled=True).astype(f32)

    half, weights = call(
        pre_along_x, [((chunk + EXTRA, both_lats), f32), ((EXTRA, both_lats), f32)], pre_in
    )
    half = lax.optimization_barrier(half.astype(f16))
    partner = lax.ppermute(half, "yh", SWAP)
    (term_half,) = call(terms_along_x, [((chunk, both_lats), f32)], terms_in, weights)
    term_half = lax.optimization_barrier(term_half.astype(f16))
    term_partner = lax.ppermute(term_half, "yh", SWAP)
    pull, weights = call(
        penalties,
        [((chunk, both_lats), f32), ((EXTRA, both_lats), f32)],
        half.astype(f32), partner.astype(f32), gates, b_both,
    )
    (grad,) = call(
        gradient,
        [((X, chunk, both_lats), bf16)],
        term_half.astype(f32), term_partner.astype(f32), weights, pull, gates,
    )
    grad = lax.all_to_all(grad, "x", 0, 0, tiled=True).reshape(wide, both_lats)
    sent, keep, away = call(
        functools.partial(backward, feats),
        [((wide, LANES), f32), ((feats + 8, lats), f32), ((feats + 8, lats), f32)],
        grad, enc_both, own_ones,
    )
    far = lax.ppermute(away, "c", SWAP)
    came = lax.all_to_all(sent.astype(f16).reshape(PEERS, rows, LANES), PLANE, 0, 0, tiled=True)
    grad_in, grad_enc, grad_bias = call(
        finish,
        [((rows, S, feats), f32), ((feats, lats), f32), ((1, lats), f32)],
        came.astype(f32).reshape(wide, LANES), keep, far,
    )
    return (grad_enc, grad_bias[0], grad_in)


def solution(mesh):
    fine = Mesh(mesh.devices.reshape(YL, Z, C, YH, X), AXES)
    return jax.shard_map(
        local,
        mesh=fine,
        in_specs=(
            P(LAT, None, TGT),
            P(TGT, LAT),
            P(LAT),
            P(None, LAT),
            P(TGT, LAT, None),
            P(TGT, LAT, None),
            P(),
        ),
        out_specs=(P(TGT, LAT), P(LAT), P(LAT, None, TGT)),
        check_vma=False,
    )
```

```python
import functools

import jax
import jax.numpy as jnp
from jax import lax
from jax.experimental import pallas as pl
from jax.experimental.pallas import tpu as pltpu
from jax.sharding import Mesh, PartitionSpec as P

S = 2
penalty = 1.0
sharpness = 1.0

YL, Z, C, YH, X = 4, 8, 2, 2, 4
AXES = ("yl", "z", "c", "yh", "x")
LAT = ("yl", "z", "c")
TGT = ("yh", "x")
PLANE = ("yl", "z")
PEERS = YL * Z
SLOTS = YH * X
LANES = 384
EXTRA = 8
PRE_SCALE = 64.0
TOP = 14.0
SWAP = [(0, 1), (1, 0)]
f32, bf16, f16 = jnp.float32, jnp.bfloat16, jnp.float16
BY_LAST = (((1,), (1,)), ((), ()))
BY_FIRST = (((0,), (0,)), ((), ()))
PARAMS = pltpu.CompilerParams(vmem_limit_bytes=24 * 1024 * 1024)


def exponent(bound):
    return jnp.ceil(jnp.log2(jnp.maximum(bound, 1e-30)))


def split_bf16(v):
    hi = lax.reduce_precision(v, 8, 7)
    mid = lax.reduce_precision(v - hi, 8, 7)
    low = lax.reduce_precision(v - hi - mid, 8, 7)
    return jnp.stack([hi, mid, low]).astype(bf16)


def call(body, outs, *args):
    shapes = [jax.ShapeDtypeStruct(*o) for o in outs]
    return pl.pallas_call(body, out_shape=shapes, compiler_params=PARAMS)(*args)


def prepare(errors_far, inputs_far, out, errors, inputs, arrived):
    fetches = [
        pltpu.make_async_copy(errors_far, errors, arrived.at[0]),
        pltpu.make_async_copy(inputs_far, inputs, arrived.at[1]),
    ]
    for fetch in fetches:
        fetch.start()
    for fetch in fetches:
        fetch.wait()
    rows, depth = errors.shape
    errs = errors[...]
    top_err = jnp.max(jnp.abs(errs.astype(f32)), axis=(0, 1), keepdims=True) * 1.01
    pad = jnp.broadcast_to(top_err, (rows, LANES - inputs.shape[2]))
    for s in range(S):
        last = jnp.concatenate([inputs[:, s, :].astype(f32), pad], axis=1).astype(bf16)
        for i in range(PEERS // S):
            out[s * (PEERS // S) + i, :, :depth] = errs
            out[s * (PEERS // S) + i, :, depth:] = last


def first(feats, last, enc_both, lines, base, out, ones_out, tops):
    wide = last.shape[0]
    chunk = wide // X
    own = last[...]
    lane = lax.broadcasted_iota(jnp.int32, own.shape, 1)
    own32 = own.astype(f32)
    ones_out[...] = jnp.where(lane < feats, own32, 1.0).astype(bf16)
    top_err = jnp.max(jnp.where(lane == feats, own32, 0.0), axis=(0, 1), keepdims=True)
    e_term = exponent(base[:, 0:1] * top_err)
    tops[...] = jnp.broadcast_to(e_term, tops.shape)
    pre = jnp.dot(own, enc_both[...], preferred_element_type=f32) * PRE_SCALE
    out[:, :chunk, :] = pre.reshape(X, chunk, enc_both.shape[1])
    row = lax.broadcasted_iota(jnp.int32, lines.shape, 0)
    extra = jnp.where(row == 3, jnp.broadcast_to(e_term, lines.shape), lines[...])
    for i in range(X):
        out[i, chunk:, :] = extra


def terms(errs, w_own, w_far, tops, base, out, w_other, arrived):
    fetch = pltpu.make_async_copy(w_far, w_other, arrived)
    fetch.start()
    lats = w_own.shape[0]
    chunk = errs.shape[0] // X
    scale = base[:, 1:2] * jnp.exp2(TOP - tops[0:1, 0:1])
    for h, w in enumerate((w_own, w_other)):
        if h == 1:
            fetch.wait()
        term = lax.dot_general(errs[...], w[...], BY_LAST, preferred_element_type=f32) * scale
        out[:, :, h * lats : (h + 1) * lats] = term.reshape(X, chunk, lats)


def pre_along_x(back, out, weights):
    at = back.shape[1] - EXTRA
    line = lambda i, k: back[i, at + k : at + k + 1, :]
    e_sq, e_term = line(0, 2), line(0, 3)
    for i in range(1, X):
        e_sq, e_term = jnp.maximum(e_sq, line(i, 2)), jnp.maximum(e_term, line(i, 3))
    e_sq, e_term = e_sq + 2.0, e_term + 2.0
    pre, squares = 0.0, 0.0
    for i in range(X):
        pre += back[i, :at, :]
        squares += (line(i, 0) + line(i, 1)) * jnp.exp2(line(i, 2) - e_sq)
        weights[i : i + 1, :] = jnp.exp2(line(i, 3) - e_term)
    weights[X:, :] = jnp.zeros((EXTRA - X, out.shape[1]), f32)
    out[:at, :] = pre
    hi = squares.astype(bf16).astype(f32)
    out[at : at + 1, :] = hi
    out[at + 1 : at + 2, :] = squares - hi
    out[at + 2 : at + 3, :] = e_sq
    out[at + 3 : at + 4, :] = e_term
    out[at + 4 :, :] = jnp.zeros((EXTRA - 4, out.shape[1]), f32)


def terms_along_x(back, weights, out):
    total = 0.0
    for i in range(X):
        total += back[i] * weights[i : i + 1, :]
    out[...] = total


def penalties(one, two, gates, bias, out, weights):
    at = gates.shape[0]
    pre, sumsq = 0.0, 0.0
    for k, half in enumerate((one, two)):
        pre += half[:at, :]
        squares = half[at : at + 1, :] + half[at + 1 : at + 2, :]
        sumsq += squares * jnp.exp2(half[at + 2 : at + 3, :] - TOP)
        weights[k : k + 1, :] = jnp.exp2(half[at + 3 : at + 4, :] - TOP)
    weights[2:, :] = jnp.zeros((EXTRA - 2, gates.shape[1]), f32)
    pre = pre * (1.0 / PRE_SCALE) + bias[...]
    norm = jnp.sqrt(sumsq)
    tanh_val = jnp.tanh(sharpness * (gates[...] * pre) * norm)
    out[...] = penalty * sharpness * norm * (1.0 - tanh_val * tanh_val)


def gradient(one, two, weights, pull, gates, out):
    dact = one[...] * weights[0:1, :] + two[...] * weights[1:2, :]
    grad = (gates[...] * (dact + pull[...])).astype(bf16)
    for i in range(X):
        out[i] = grad


def backward(feats, grad, enc_both, own_ones, sent, keep, away):
    lats = keep.shape[1]
    part = lax.dot_general(grad[...], enc_both[...], BY_LAST, preferred_element_type=f32)
    e_part = exponent(jnp.max(jnp.abs(part), axis=(0, 1), keepdims=True))
    lane = lax.broadcasted_iota(jnp.int32, part.shape, 1)
    sent[...] = jnp.where(lane < feats, part * jnp.exp2(TOP - e_part), jnp.broadcast_to(e_part, part.shape))
    enc = lax.dot_general(own_ones[...], grad[...], BY_FIRST, preferred_element_type=f32)
    keep[...] = enc[: keep.shape[0], :lats]
    away[...] = enc[: away.shape[0], lats:]


def finish(came, keep, far, grad_in, grad_enc, grad_bias):
    rows, _, feats = grad_in.shape
    values = came[:, :feats] * jnp.exp2(came[:, feats : feats + 1] - TOP)
    values = values.reshape(S, PEERS // S, rows, feats)
    for s in range(S):
        grad_in[:, s, :] = jnp.sum(values[s], axis=0)
    both = keep[...] + far[...]
    grad_enc[...] = both[:feats]
    grad_bias[...] = both[feats : feats + 1]


def local(inputs, w_enc, b_enc, masks, w_dec, errors, target_of):
    yl, core = lax.axis_index("yl"), lax.axis_index("c")
    x = lax.axis_index("x")
    slot = lax.axis_index("yh") * X + x
    source = yl * S // YL
    feats, lats = w_enc.shape
    depth = w_dec.shape[2]
    rows = inputs.shape[0]
    wide = PEERS * rows
    chunk = wide // X
    both_lats = C * lats
    pad = LANES - feats

    held = pl.pallas_call(
        prepare,
        out_shape=pltpu.HBM((PEERS, rows, depth + LANES), bf16),
        in_specs=[pl.BlockSpec(memory_space=pltpu.HBM)] * 2,
        scratch_shapes=[
            pltpu.VMEM(errors.shape[1:], bf16),
            pltpu.VMEM(inputs.shape, bf16),
            pltpu.SemaphoreType.DMA((2,)),
        ],
        compiler_params=PARAMS,
    )(*(pltpu.with_memory_space_constraint(v, pltpu.HBM) for v in (errors[0], inputs)))
    held, masks, w_dec = lax.optimization_barrier((held, masks, w_dec))
    got = lax.all_to_all(held, PLANE, 0, 0, tiled=True).reshape(wide, depth + LANES)

    gates6 = masks.reshape(X, chunk // rows, C, rows, lats)
    gates5 = lax.dynamic_index_in_dim(gates6, x, 0, keepdims=False)
    gates_own = lax.dynamic_index_in_dim(gates5, core, 1, keepdims=False).reshape(chunk, lats)
    gates_send = lax.dynamic_index_in_dim(gates5, 1 - core, 1, keepdims=False).reshape(chunk, lats)
    w_own = w_dec[0]
    square = jnp.einsum("cd,cd->c", w_own, w_own, preferred_element_type=f32)
    pack = jnp.concatenate(
        [
            w_enc,
            jnp.zeros((pad, lats), bf16),
            gates_send.astype(bf16),
            split_bf16(b_enc),
            split_bf16(square),
            jnp.zeros((10, lats), bf16),
        ],
        axis=0,
    )
    pack_other = lax.ppermute(pack, "c", SWAP)
    w_late, pack_other = lax.optimization_barrier((w_own, pack_other))
    w_other = lax.ppermute(w_late, "c", SWAP)
    enc_both = jnp.concatenate([pack[:LANES], pack_other[:LANES]], axis=1)
    gates_other = pack_other[LANES : LANES + chunk].astype(f32)
    gates = jnp.concatenate([gates_own.astype(f32), gates_other], axis=1)
    parts = jnp.sum(pack_other[LANES + chunk : LANES + chunk + 6].astype(f32).reshape(2, 3, lats), axis=1)
    b_both = jnp.concatenate([b_enc, parts[0]])[None]

    slots = jnp.arange(target_of.shape[0], dtype=jnp.int32)
    layer = jnp.sum(jnp.where(slots == slot, target_of, 0))
    flag = (layer >= source).astype(f32)
    squares = flag * jnp.concatenate([square, parts[1]])
    top_sq = jnp.max(squares)
    e_sq = exponent(top_sq)
    scaled = squares * jnp.exp2(TOP - e_sq)
    hi = lax.reduce_precision(scaled, 5, 10)
    lines = jnp.concatenate(
        [
            hi[None],
            (scaled - hi)[None],
            jnp.broadcast_to(e_sq, (1, both_lats)),
            jnp.zeros((EXTRA - 3, both_lats), f32),
        ],
        axis=0,
    )
    base = jnp.stack([jnp.sqrt(depth * 1.01 * top_sq), flag])[None]
    lines, base, enc_both, gates, b_both, got = lax.optimization_barrier(
        (lines, base, enc_both, gates, b_both, got)
    )

    whole = lambda shape: pl.BlockSpec(shape, lambda i: (0,) * len(shape))
    pre_out, own_ones, tops = pl.pallas_call(
        functools.partial(first, feats),
        grid=(1,),
        in_specs=[
            pl.BlockSpec((wide, LANES), lambda i: (0, depth // LANES)),
            whole((LANES, both_lats)),
            whole((EXTRA, both_lats)),
            whole((1, 2)),
        ],
        out_specs=[whole((X, chunk + EXTRA, both_lats)), whole((wide, LANES)), whole((EXTRA, 128))],
        out_shape=[
            jax.ShapeDtypeStruct((X, chunk + EXTRA, both_lats), f32),
            jax.ShapeDtypeStruct((wide, LANES), bf16),
            jax.ShapeDtypeStruct((EXTRA, 128), f32),
        ],
        compiler_params=PARAMS,
    )(got, enc_both, lines, base)
    pre_in = lax.all_to_all(pre_out.astype(f16), "x", 0, 0, tiled=True).astype(f32)
    term = pl.pallas_call(
        terms,
        grid=(1,),
        in_specs=[
            whole((wide, depth)),
            whole((lats, depth)),
            pl.BlockSpec(memory_space=pl.ANY),
            whole((EXTRA, 128)),
            whole((1, 2)),
        ],
        out_specs=whole((X, chunk, both_lats)),
        out_shape=jax.ShapeDtypeStruct((X, chunk, both_lats), f32),
        scratch_shapes=[pltpu.VMEM((lats, depth), bf16), pltpu.SemaphoreType.DMA],
        compiler_params=PARAMS,
        cost_estimate=pl.CostEstimate(
            flops=2 * wide * depth * both_lats,
            bytes_accessed=2 * (wide + both_lats) * depth + 4 * wide * both_lats,
            transcendentals=0,
        ),
    )(got, w_own, w_other, tops, base)
    terms_in = lax.all_to_all(term.astype(f16), "x", 0, 0, tiled=True).astype(f32)

    half, weights = call(
        pre_along_x, [((chunk + EXTRA, both_lats), f32), ((EXTRA, both_lats), f32)], pre_in
    )
    half = lax.optimization_barrier(half.astype(f16))
    partner = lax.ppermute(half, "yh", SWAP)
    (term_half,) = call(terms_along_x, [((chunk, both_lats), f32)], terms_in, weights)
    term_half = lax.optimization_barrier(term_half.astype(f16))
    term_partner = lax.ppermute(term_half, "yh", SWAP)
    pull, weights = call(
        penalties,
        [((chunk, both_lats), f32), ((EXTRA, both_lats), f32)],
        half.astype(f32), partner.astype(f32), gates, b_both,
    )
    (grad,) = call(
        gradient,
        [((X, chunk, both_lats), bf16)],
        term_half.astype(f32), term_partner.astype(f32), weights, pull, gates,
    )
    grad = lax.all_to_all(grad, "x", 0, 0, tiled=True).reshape(wide, both_lats)
    sent, keep, away = call(
        functools.partial(backward, feats),
        [((wide, LANES), f32), ((feats + 8, lats), f32), ((feats + 8, lats), f32)],
        grad, enc_both, own_ones,
    )
    far = lax.ppermute(away, "c", SWAP)
    came = lax.all_to_all(sent.astype(f16).reshape(PEERS, rows, LANES), PLANE, 0, 0, tiled=True)
    grad_in, grad_enc, grad_bias = call(
        finish,
        [((rows, S, feats), f32), ((feats, lats), f32), ((1, lats), f32)],
        came.astype(f32).reshape(wide, LANES), keep, far,
    )
    return (grad_enc, grad_bias[0], grad_in)


def solution(mesh):
    fine = Mesh(mesh.devices.reshape(YL, Z, C, YH, X), AXES)
    return jax.shard_map(
        local,
        mesh=fine,
        in_specs=(
            P(LAT, None, TGT),
            P(TGT, LAT),
            P(LAT),
            P(None, LAT),
            P(TGT, LAT, None),
            P(TGT, LAT, None),
            P(),
        ),
        out_specs=(P(TGT, LAT), P(LAT), P(LAT, None, TGT)),
        check_vma=False,
    )
```

```python
import functools

import jax
import jax.numpy as jnp
from jax import lax
from jax.experimental import pallas as pl
from jax.experimental.pallas import tpu as pltpu
from jax.sharding import Mesh, PartitionSpec as P

S = 2
penalty = 1.0
sharpness = 1.0

YL, Z, C, YH, X = 4, 8, 2, 2, 4
AXES = ("yl", "z", "c", "yh", "x")
LAT = ("yl", "z", "c")
TGT = ("yh", "x")
PLANE = ("yl", "z")
PEERS = YL * Z
SLOTS = YH * X
LANES = 384
EXTRA = 8
PRE_SCALE = 64.0
TOP = 14.0
SWAP = [(0, 1), (1, 0)]
f32, bf16, f16 = jnp.float32, jnp.bfloat16, jnp.float16
BY_LAST = (((1,), (1,)), ((), ()))
BY_FIRST = (((0,), (0,)), ((), ()))
PARAMS = pltpu.CompilerParams(vmem_limit_bytes=24 * 1024 * 1024)


def exponent(bound):
    return jnp.ceil(jnp.log2(jnp.maximum(bound, 1e-30)))


def split_bf16(v):
    hi = lax.reduce_precision(v, 8, 7)
    mid = lax.reduce_precision(v - hi, 8, 7)
    low = lax.reduce_precision(v - hi - mid, 8, 7)
    return jnp.stack([hi, mid, low]).astype(bf16)


def call(body, outs, *args):
    shapes = [jax.ShapeDtypeStruct(*o) for o in outs]
    return pl.pallas_call(body, out_shape=shapes, compiler_params=PARAMS)(*args)


def prepare(errors_far, inputs_far, out, errors, inputs, arrived):
    fetches = [
        pltpu.make_async_copy(errors_far, errors, arrived.at[0]),
        pltpu.make_async_copy(inputs_far, inputs, arrived.at[1]),
    ]
    for fetch in fetches:
        fetch.start()
    for fetch in fetches:
        fetch.wait()
    rows, depth = errors.shape
    errs = errors[...]
    top_err = jnp.max(jnp.abs(errs.astype(f32)), axis=(0, 1), keepdims=True) * 1.01
    pad = jnp.broadcast_to(top_err, (rows, LANES - inputs.shape[2]))
    for s in range(S):
        last = jnp.concatenate([inputs[:, s, :].astype(f32), pad], axis=1).astype(bf16)
        for i in range(PEERS // S):
            out[s * (PEERS // S) + i, :, :depth] = errs
            out[s * (PEERS // S) + i, :, depth:] = last


def first(feats, last, enc_both, lines, base, out, ones_out, tops):
    wide = last.shape[0]
    chunk = wide // X
    own = last[...]
    lane = lax.broadcasted_iota(jnp.int32, own.shape, 1)
    own32 = own.astype(f32)
    ones_out[...] = jnp.where(lane < feats, own32, 1.0).astype(bf16)
    top_err = jnp.max(jnp.where(lane == feats, own32, 0.0), axis=(0, 1), keepdims=True)
    e_term = exponent(base[:, 0:1] * top_err)
    tops[...] = jnp.broadcast_to(e_term, tops.shape)
    pre = jnp.dot(own, enc_both[...], preferred_element_type=f32) * PRE_SCALE
    out[:, :chunk, :] = pre.reshape(X, chunk, enc_both.shape[1])
    row = lax.broadcasted_iota(jnp.int32, lines.shape, 0)
    extra = jnp.where(row == 3, jnp.broadcast_to(e_term, lines.shape), lines[...])
    for i in range(X):
        out[i, chunk:, :] = extra


def terms(errs, w_own, w_far, tops, base, out, w_other, arrived):
    fetch = pltpu.make_async_copy(w_far, w_other, arrived)
    fetch.start()
    lats = w_own.shape[0]
    chunk = errs.shape[0] // X
    scale = base[:, 1:2] * jnp.exp2(TOP - tops[0:1, 0:1])
    for h, w in enumerate((w_own, w_other)):
        if h == 1:
            fetch.wait()
        term = lax.dot_general(errs[...], w[...], BY_LAST, preferred_element_type=f32) * scale
        out[:, :, h * lats : (h + 1) * lats] = term.reshape(X, chunk, lats)


def pre_along_x(back, out, weights):
    at = back.shape[1] - EXTRA
    line = lambda i, k: back[i, at + k : at + k + 1, :]
    e_sq, e_term = line(0, 2), line(0, 3)
    for i in range(1, X):
        e_sq, e_term = jnp.maximum(e_sq, line(i, 2)), jnp.maximum(e_term, line(i, 3))
    e_sq, e_term = e_sq + 2.0, e_term + 2.0
    pre, squares = 0.0, 0.0
    for i in range(X):
        pre += back[i, :at, :]
        squares += (line(i, 0) + line(i, 1)) * jnp.exp2(line(i, 2) - e_sq)
        weights[i : i + 1, :] = jnp.exp2(line(i, 3) - e_term)
    weights[X:, :] = jnp.zeros((EXTRA - X, out.shape[1]), f32)
    out[:at, :] = pre
    hi = squares.astype(bf16).astype(f32)
    out[at : at + 1, :] = hi
    out[at + 1 : at + 2, :] = squares - hi
    out[at + 2 : at + 3, :] = e_sq
    out[at + 3 : at + 4, :] = e_term
    out[at + 4 :, :] = jnp.zeros((EXTRA - 4, out.shape[1]), f32)


def penalties(one, two, gates, bias, out, weights):
    at = gates.shape[0]
    pre, sumsq = 0.0, 0.0
    for k, half in enumerate((one, two)):
        pre += half[:at, :]
        squares = half[at : at + 1, :] + half[at + 1 : at + 2, :]
        sumsq += squares * jnp.exp2(half[at + 2 : at + 3, :] - TOP)
        weights[k : k + 1, :] = jnp.exp2(half[at + 3 : at + 4, :] - TOP)
    weights[2:, :] = jnp.zeros((EXTRA - 2, gates.shape[1]), f32)
    pre = pre * (1.0 / PRE_SCALE) + bias[...]
    norm = jnp.sqrt(sumsq)
    tanh_val = jnp.tanh(sharpness * (gates[...] * pre) * norm)
    out[...] = penalty * sharpness * norm * (1.0 - tanh_val * tanh_val)


def gradient(one, two, weights, pull, gates, out):
    dact = one[...] * weights[0:1, :] + two[...] * weights[1:2, :]
    grad = (gates[...] * (dact + pull[...])).astype(bf16)
    for i in range(X):
        out[i] = grad


def backward(feats, grad, enc_both, own_ones, sent, keep, away):
    lats = keep.shape[1]
    part = lax.dot_general(grad[...], enc_both[...], BY_LAST, preferred_element_type=f32)
    e_part = exponent(jnp.max(jnp.abs(part), axis=(0, 1), keepdims=True))
    lane = lax.broadcasted_iota(jnp.int32, part.shape, 1)
    sent[...] = jnp.where(lane < feats, part * jnp.exp2(TOP - e_part), jnp.broadcast_to(e_part, part.shape))
    enc = lax.dot_general(own_ones[...], grad[...], BY_FIRST, preferred_element_type=f32)
    keep[...] = enc[: keep.shape[0], :lats]
    away[...] = enc[: away.shape[0], lats:]


def finish(came, keep, far, grad_in, grad_enc, grad_bias):
    rows, _, feats = grad_in.shape
    values = came[:, :feats] * jnp.exp2(came[:, feats : feats + 1] - TOP)
    values = values.reshape(S, PEERS // S, rows, feats)
    for s in range(S):
        grad_in[:, s, :] = jnp.sum(values[s], axis=0)
    both = keep[...] + far[...]
    grad_enc[...] = both[:feats]
    grad_bias[...] = both[feats : feats + 1]


def local(inputs, w_enc, b_enc, masks, w_dec, errors, target_of):
    yl, core = lax.axis_index("yl"), lax.axis_index("c")
    x = lax.axis_index("x")
    slot = lax.axis_index("yh") * X + x
    source = yl * S // YL
    feats, lats = w_enc.shape
    depth = w_dec.shape[2]
    rows = inputs.shape[0]
    wide = PEERS * rows
    chunk = wide // X
    both_lats = C * lats
    pad = LANES - feats

    held = pl.pallas_call(
        prepare,
        out_shape=pltpu.HBM((PEERS, rows, depth + LANES), bf16),
        in_specs=[pl.BlockSpec(memory_space=pltpu.HBM)] * 2,
        scratch_shapes=[
            pltpu.VMEM(errors.shape[1:], bf16),
            pltpu.VMEM(inputs.shape, bf16),
            pltpu.SemaphoreType.DMA((2,)),
        ],
        compiler_params=PARAMS,
    )(*(pltpu.with_memory_space_constraint(v, pltpu.HBM) for v in (errors[0], inputs)))
    held, masks, w_dec = lax.optimization_barrier((held, masks, w_dec))
    got = lax.all_to_all(held, PLANE, 0, 0, tiled=True).reshape(wide, depth + LANES)

    gates6 = masks.reshape(X, chunk // rows, C, rows, lats)
    gates5 = lax.dynamic_index_in_dim(gates6, x, 0, keepdims=False)
    gates_own = lax.dynamic_index_in_dim(gates5, core, 1, keepdims=False).reshape(chunk, lats)
    gates_send = lax.dynamic_index_in_dim(gates5, 1 - core, 1, keepdims=False).reshape(chunk, lats)
    w_own = w_dec[0]
    square = jnp.einsum("cd,cd->c", w_own, w_own, preferred_element_type=f32)
    pack = jnp.concatenate(
        [
            w_enc,
            jnp.zeros((pad, lats), bf16),
            gates_send.astype(bf16),
            split_bf16(b_enc),
            split_bf16(square),
            jnp.zeros((10, lats), bf16),
        ],
        axis=0,
    )
    pack_other = lax.ppermute(pack, "c", SWAP)
    w_late, pack_other = lax.optimization_barrier((w_own, pack_other))
    w_other = lax.ppermute(w_late, "c", SWAP)
    enc_both = jnp.concatenate([pack[:LANES], pack_other[:LANES]], axis=1)
    gates_other = pack_other[LANES : LANES + chunk].astype(f32)
    gates = jnp.concatenate([gates_own.astype(f32), gates_other], axis=1)
    parts = jnp.sum(pack_other[LANES + chunk : LANES + chunk + 6].astype(f32).reshape(2, 3, lats), axis=1)
    b_both = jnp.concatenate([b_enc, parts[0]])[None]

    slots = jnp.arange(target_of.shape[0], dtype=jnp.int32)
    layer = jnp.sum(jnp.where(slots == slot, target_of, 0))
    flag = (layer >= source).astype(f32)
    squares = flag * jnp.concatenate([square, parts[1]])
    top_sq = jnp.max(squares)
    e_sq = exponent(top_sq)
    scaled = squares * jnp.exp2(TOP - e_sq)
    hi = lax.reduce_precision(scaled, 5, 10)
    lines = jnp.concatenate(
        [
            hi[None],
            (scaled - hi)[None],
            jnp.broadcast_to(e_sq, (1, both_lats)),
            jnp.zeros((EXTRA - 3, both_lats), f32),
        ],
        axis=0,
    )
    base = jnp.stack([jnp.sqrt(depth * 1.01 * top_sq), flag])[None]
    lines, base, enc_both, gates, b_both, got = lax.optimization_barrier(
        (lines, base, enc_both, gates, b_both, got)
    )

    whole = lambda shape: pl.BlockSpec(shape, lambda i: (0,) * len(shape))
    pre_out, own_ones, tops = pl.pallas_call(
        functools.partial(first, feats),
        grid=(1,),
        in_specs=[
            pl.BlockSpec((wide, LANES), lambda i: (0, depth // LANES)),
            whole((LANES, both_lats)),
            whole((EXTRA, both_lats)),
            whole((1, 2)),
        ],
        out_specs=[whole((X, chunk + EXTRA, both_lats)), whole((wide, LANES)), whole((EXTRA, 128))],
        out_shape=[
            jax.ShapeDtypeStruct((X, chunk + EXTRA, both_lats), f32),
            jax.ShapeDtypeStruct((wide, LANES), bf16),
            jax.ShapeDtypeStruct((EXTRA, 128), f32),
        ],
        compiler_params=PARAMS,
    )(got, enc_both, lines, base)
    pre_in = lax.all_to_all(pre_out.astype(f16), "x", 0, 0, tiled=True).astype(f32)
    term = pl.pallas_call(
        terms,
        grid=(1,),
        in_specs=[
            whole((wide, depth)),
            whole((lats, depth)),
            pl.BlockSpec(memory_space=pl.ANY),
            whole((EXTRA, 128)),
            whole((1, 2)),
        ],
        out_specs=whole((X, chunk, both_lats)),
        out_shape=jax.ShapeDtypeStruct((X, chunk, both_lats), f32),
        scratch_shapes=[pltpu.VMEM((lats, depth), bf16), pltpu.SemaphoreType.DMA],
        compiler_params=PARAMS,
        cost_estimate=pl.CostEstimate(
            flops=2 * wide * depth * both_lats,
            bytes_accessed=2 * (wide + both_lats) * depth + 4 * wide * both_lats,
            transcendentals=0,
        ),
    )(got, w_own, w_other, tops, base)
    terms_in = lax.all_to_all(term.astype(f16), "x", 0, 0, tiled=True)

    half, weights = call(
        pre_along_x, [((chunk + EXTRA, both_lats), f32), ((EXTRA, both_lats), f32)], pre_in
    )
    half = lax.optimization_barrier(half.astype(f16))
    partner = lax.ppermute(half, "yh", SWAP)
    term_half = jnp.sum(terms_in.astype(f32) * weights[:X, None, :], axis=0)
    term_half = lax.optimization_barrier(term_half.astype(f16))
    term_partner = lax.ppermute(term_half, "yh", SWAP)
    pull, weights = call(
        penalties,
        [((chunk, both_lats), f32), ((EXTRA, both_lats), f32)],
        half.astype(f32), partner.astype(f32), gates, b_both,
    )
    (grad,) = call(
        gradient,
        [((X, chunk, both_lats), bf16)],
        term_half.astype(f32), term_partner.astype(f32), weights, pull, gates,
    )
    grad = lax.all_to_all(grad, "x", 0, 0, tiled=True).reshape(wide, both_lats)
    sent, keep, away = call(
        functools.partial(backward, feats),
        [((wide, LANES), f32), ((feats + 8, lats), f32), ((feats + 8, lats), f32)],
        grad, enc_both, own_ones,
    )
    far = lax.ppermute(away, "c", SWAP)
    came = lax.all_to_all(sent.astype(f16).reshape(PEERS, rows, LANES), PLANE, 0, 0, tiled=True)
    grad_in, grad_enc, grad_bias = call(
        finish,
        [((rows, S, feats), f32), ((feats, lats), f32), ((1, lats), f32)],
        came.astype(f32).reshape(wide, LANES), keep, far,
    )
    return (grad_enc, grad_bias[0], grad_in)


def solution(mesh):
    fine = Mesh(mesh.devices.reshape(YL, Z, C, YH, X), AXES)
    return jax.shard_map(
        local,
        mesh=fine,
        in_specs=(
            P(LAT, None, TGT),
            P(TGT, LAT),
            P(LAT),
            P(None, LAT),
            P(TGT, LAT, None),
            P(TGT, LAT, None),
            P(),
        ),
        out_specs=(P(TGT, LAT), P(LAT), P(LAT, None, TGT)),
        check_vma=False,
    )
```

```python
import functools

import jax
import jax.numpy as jnp
from jax import lax
from jax.experimental import pallas as pl
from jax.experimental.pallas import tpu as pltpu
from jax.sharding import Mesh, PartitionSpec as P

S = 2
penalty = 1.0
sharpness = 1.0

YL, Z, C, YH, X = 4, 8, 2, 2, 4
AXES = ("yl", "z", "c", "yh", "x")
LAT = ("yl", "z", "c")
TGT = ("yh", "x")
PLANE = ("yl", "z")
PEERS = YL * Z
SLOTS = YH * X
LANES = 384
EXTRA = 8
PRE_SCALE = 64.0
TOP = 14.0
SWAP = [(0, 1), (1, 0)]
f32, bf16, f16 = jnp.float32, jnp.bfloat16, jnp.float16
BY_LAST = (((1,), (1,)), ((), ()))
BY_FIRST = (((0,), (0,)), ((), ()))
PARAMS = pltpu.CompilerParams(vmem_limit_bytes=24 * 1024 * 1024)


def exponent(bound):
    return jnp.ceil(jnp.log2(jnp.maximum(bound, 1e-30)))


def split_bf16(v):
    hi = lax.reduce_precision(v, 8, 7)
    mid = lax.reduce_precision(v - hi, 8, 7)
    low = lax.reduce_precision(v - hi - mid, 8, 7)
    return jnp.stack([hi, mid, low]).astype(bf16)


def call(body, outs, *args):
    shapes = [jax.ShapeDtypeStruct(*o) for o in outs]
    return pl.pallas_call(body, out_shape=shapes, compiler_params=PARAMS)(*args)


def prepare(errors_far, inputs_far, out, errors, inputs, arrived):
    fetches = [
        pltpu.make_async_copy(errors_far, errors, arrived.at[0]),
        pltpu.make_async_copy(inputs_far, inputs, arrived.at[1]),
    ]
    for fetch in fetches:
        fetch.start()
    for fetch in fetches:
        fetch.wait()
    rows, depth = errors.shape
    errs = errors[...]
    top_err = jnp.max(jnp.abs(errs.astype(f32)), axis=(0, 1), keepdims=True) * 1.01
    pad = jnp.broadcast_to(top_err, (rows, LANES - inputs.shape[2]))
    for s in range(S):
        last = jnp.concatenate([inputs[:, s, :].astype(f32), pad], axis=1).astype(bf16)
        for i in range(PEERS // S):
            out[s * (PEERS // S) + i, :, :depth] = errs
            out[s * (PEERS // S) + i, :, depth:] = last


def first(feats, last, enc_both, lines, base, out, ones_out, tops):
    wide = last.shape[0]
    chunk = wide // X
    own = last[...]
    lane = lax.broadcasted_iota(jnp.int32, own.shape, 1)
    own32 = own.astype(f32)
    ones_out[...] = jnp.where(lane < feats, own32, 1.0).astype(bf16)
    top_err = jnp.max(jnp.where(lane == feats, own32, 0.0), axis=(0, 1), keepdims=True)
    e_term = exponent(base[:, 0:1] * top_err)
    tops[...] = jnp.broadcast_to(e_term, tops.shape)
    pre = jnp.dot(own, enc_both[...], preferred_element_type=f32) * PRE_SCALE
    out[:, :chunk, :] = pre.reshape(X, chunk, enc_both.shape[1])
    row = lax.broadcasted_iota(jnp.int32, lines.shape, 0)
    extra = jnp.where(row == 3, jnp.broadcast_to(e_term, lines.shape), lines[...])
    for i in range(X):
        out[i, chunk:, :] = extra


def terms(errs, w_own, w_far, tops, base, out, w_other, arrived):
    fetch = pltpu.make_async_copy(w_far, w_other, arrived)
    fetch.start()
    lats = w_own.shape[0]
    chunk = errs.shape[0] // X
    scale = base[:, 1:2] * jnp.exp2(TOP - tops[0:1, 0:1])
    for h, w in enumerate((w_own, w_other)):
        if h == 1:
            fetch.wait()
        term = lax.dot_general(errs[...], w[...], BY_LAST, preferred_element_type=f32) * scale
        out[:, :, h * lats : (h + 1) * lats] = term.reshape(X, chunk, lats)


def pre_along_x(back, out, weights):
    at = back.shape[1] - EXTRA
    line = lambda i, k: back[i, at + k : at + k + 1, :]
    e_sq, e_term = line(0, 2), line(0, 3)
    for i in range(1, X):
        e_sq, e_term = jnp.maximum(e_sq, line(i, 2)), jnp.maximum(e_term, line(i, 3))
    e_sq, e_term = e_sq + 2.0, e_term + 2.0
    pre, squares = 0.0, 0.0
    for i in range(X):
        pre += back[i, :at, :]
        squares += (line(i, 0) + line(i, 1)) * jnp.exp2(line(i, 2) - e_sq)
        weights[i : i + 1, :] = jnp.exp2(line(i, 3) - e_term)
    out[:at, :] = pre
    hi = squares.astype(bf16).astype(f32)
    out[at : at + 1, :] = hi
    out[at + 1 : at + 2, :] = squares - hi
    out[at + 2 : at + 3, :] = e_sq
    out[at + 3 : at + 4, :] = e_term
    out[at + 4 :, :] = jnp.zeros((EXTRA - 4, out.shape[1]), f32)


def penalties(one, two, gates, bias, out, weights):
    at = gates.shape[0]
    pre, sumsq = 0.0, 0.0
    for k, half in enumerate((one, two)):
        pre += half[:at, :]
        squares = half[at : at + 1, :] + half[at + 1 : at + 2, :]
        sumsq += squares * jnp.exp2(half[at + 2 : at + 3, :] - TOP)
        weights[k : k + 1, :] = jnp.exp2(half[at + 3 : at + 4, :] - TOP)
    weights[2:, :] = jnp.zeros((EXTRA - 2, gates.shape[1]), f32)
    pre = pre * (1.0 / PRE_SCALE) + bias[...]
    norm = jnp.sqrt(sumsq)
    tanh_val = jnp.tanh(sharpness * (gates[...] * pre) * norm)
    out[...] = penalty * sharpness * norm * (1.0 - tanh_val * tanh_val)


def gradient(one, two, weights, pull, gates, out):
    dact = one[...] * weights[0:1, :] + two[...] * weights[1:2, :]
    grad = (gates[...] * (dact + pull[...])).astype(bf16)
    for i in range(X):
        out[i] = grad


def backward(feats, grad, enc_both, own_ones, sent, keep, away):
    lats = keep.shape[1]
    part = lax.dot_general(grad[...], enc_both[...], BY_LAST, preferred_element_type=f32)
    e_part = exponent(jnp.max(jnp.abs(part), axis=(0, 1), keepdims=True))
    lane = lax.broadcasted_iota(jnp.int32, part.shape, 1)
    sent[...] = jnp.where(lane < feats, part * jnp.exp2(TOP - e_part), jnp.broadcast_to(e_part, part.shape))
    enc = lax.dot_general(own_ones[...], grad[...], BY_FIRST, preferred_element_type=f32)
    keep[...] = enc[: keep.shape[0], :lats]
    away[...] = enc[: away.shape[0], lats:]


def finish(came, keep, far, grad_in, grad_enc, grad_bias):
    rows, _, feats = grad_in.shape
    values = came[:, :feats] * jnp.exp2(came[:, feats : feats + 1] - TOP)
    values = values.reshape(S, PEERS // S, rows, feats)
    for s in range(S):
        grad_in[:, s, :] = jnp.sum(values[s], axis=0)
    both = keep[...] + far[...]
    grad_enc[...] = both[:feats]
    grad_bias[...] = both[feats : feats + 1]


def local(inputs, w_enc, b_enc, masks, w_dec, errors, target_of):
    yl, core = lax.axis_index("yl"), lax.axis_index("c")
    x = lax.axis_index("x")
    slot = lax.axis_index("yh") * X + x
    source = yl * S // YL
    feats, lats = w_enc.shape
    depth = w_dec.shape[2]
    rows = inputs.shape[0]
    wide = PEERS * rows
    chunk = wide // X
    both_lats = C * lats
    pad = LANES - feats

    held = pl.pallas_call(
        prepare,
        out_shape=pltpu.HBM((PEERS, rows, depth + LANES), bf16),
        in_specs=[pl.BlockSpec(memory_space=pltpu.HBM)] * 2,
        scratch_shapes=[
            pltpu.VMEM(errors.shape[1:], bf16),
            pltpu.VMEM(inputs.shape, bf16),
            pltpu.SemaphoreType.DMA((2,)),
        ],
        compiler_params=PARAMS,
    )(*(pltpu.with_memory_space_constraint(v, pltpu.HBM) for v in (errors[0], inputs)))
    held, masks, w_dec = lax.optimization_barrier((held, masks, w_dec))
    got = lax.all_to_all(held, PLANE, 0, 0, tiled=True).reshape(wide, depth + LANES)

    gates6 = masks.reshape(X, chunk // rows, C, rows, lats)
    gates5 = lax.dynamic_index_in_dim(gates6, x, 0, keepdims=False)
    gates_own = lax.dynamic_index_in_dim(gates5, core, 1, keepdims=False).reshape(chunk, lats)
    gates_send = lax.dynamic_index_in_dim(gates5, 1 - core, 1, keepdims=False).reshape(chunk, lats)
    w_own = w_dec[0]
    square = jnp.einsum("cd,cd->c", w_own, w_own, preferred_element_type=f32)
    pack = jnp.concatenate(
        [
            w_enc,
            jnp.zeros((pad, lats), bf16),
            gates_send.astype(bf16),
            split_bf16(b_enc),
            split_bf16(square),
            jnp.zeros((10, lats), bf16),
        ],
        axis=0,
    )
    pack_other = lax.ppermute(pack, "c", SWAP)
    w_late, pack_other = lax.optimization_barrier((w_own, pack_other))
    w_other = lax.ppermute(w_late, "c", SWAP)
    enc_both = jnp.concatenate([pack[:LANES], pack_other[:LANES]], axis=1)
    gates_other = pack_other[LANES : LANES + chunk].astype(f32)
    gates = jnp.concatenate([gates_own.astype(f32), gates_other], axis=1)
    parts = jnp.sum(pack_other[LANES + chunk : LANES + chunk + 6].astype(f32).reshape(2, 3, lats), axis=1)
    b_both = jnp.concatenate([b_enc, parts[0]])[None]

    slots = jnp.arange(target_of.shape[0], dtype=jnp.int32)
    layer = jnp.sum(jnp.where(slots == slot, target_of, 0))
    flag = (layer >= source).astype(f32)
    squares = flag * jnp.concatenate([square, parts[1]])
    top_sq = jnp.max(squares)
    e_sq = exponent(top_sq)
    scaled = squares * jnp.exp2(TOP - e_sq)
    hi = lax.reduce_precision(scaled, 5, 10)
    lines = jnp.concatenate(
        [
            hi[None],
            (scaled - hi)[None],
            jnp.broadcast_to(e_sq, (1, both_lats)),
            jnp.zeros((EXTRA - 3, both_lats), f32),
        ],
        axis=0,
    )
    base = jnp.stack([jnp.sqrt(depth * 1.01 * top_sq), flag])[None]
    lines, base, enc_both, gates, b_both, got = lax.optimization_barrier(
        (lines, base, enc_both, gates, b_both, got)
    )

    whole = lambda shape: pl.BlockSpec(shape, lambda i: (0,) * len(shape))
    pre_out, own_ones, tops = pl.pallas_call(
        functools.partial(first, feats),
        grid=(1,),
        in_specs=[
            pl.BlockSpec((wide, LANES), lambda i: (0, depth // LANES)),
            whole((LANES, both_lats)),
            whole((EXTRA, both_lats)),
            whole((1, 2)),
        ],
        out_specs=[whole((X, chunk + EXTRA, both_lats)), whole((wide, LANES)), whole((EXTRA, 128))],
        out_shape=[
            jax.ShapeDtypeStruct((X, chunk + EXTRA, both_lats), f32),
            jax.ShapeDtypeStruct((wide, LANES), bf16),
            jax.ShapeDtypeStruct((EXTRA, 128), f32),
        ],
        compiler_params=PARAMS,
    )(got, enc_both, lines, base)
    pre_in = lax.all_to_all(pre_out.astype(f16), "x", 0, 0, tiled=True).astype(f32)
    term = pl.pallas_call(
        terms,
        grid=(1,),
        in_specs=[
            whole((wide, depth)),
            whole((lats, depth)),
            pl.BlockSpec(memory_space=pl.ANY),
            whole((EXTRA, 128)),
            whole((1, 2)),
        ],
        out_specs=whole((X, chunk, both_lats)),
        out_shape=jax.ShapeDtypeStruct((X, chunk, both_lats), f32),
        scratch_shapes=[pltpu.VMEM((lats, depth), bf16), pltpu.SemaphoreType.DMA],
        compiler_params=PARAMS,
        cost_estimate=pl.CostEstimate(
            flops=2 * wide * depth * both_lats,
            bytes_accessed=2 * (wide + both_lats) * depth + 4 * wide * both_lats,
            transcendentals=0,
        ),
    )(got, w_own, w_other, tops, base)
    terms_in = lax.all_to_all(term.astype(f16), "x", 0, 0, tiled=True)

    half, weights = call(
        pre_along_x, [((chunk + EXTRA, both_lats), f32), ((X, both_lats), f32)], pre_in
    )
    half = lax.optimization_barrier(half.astype(f16))
    partner = lax.ppermute(half, "yh", SWAP)
    term_half = jnp.sum(terms_in.astype(f32) * weights[:, None, :], axis=0)
    term_half = lax.optimization_barrier(term_half.astype(f16))
    term_partner = lax.ppermute(term_half, "yh", SWAP)
    pull, weights = call(
        penalties,
        [((chunk, both_lats), f32), ((EXTRA, both_lats), f32)],
        half.astype(f32), partner.astype(f32), gates, b_both,
    )
    (grad,) = call(
        gradient,
        [((X, chunk, both_lats), bf16)],
        term_half.astype(f32), term_partner.astype(f32), weights, pull, gates,
    )
    grad = lax.all_to_all(grad, "x", 0, 0, tiled=True).reshape(wide, both_lats)
    sent, keep, away = call(
        functools.partial(backward, feats),
        [((wide, LANES), f32), ((feats + 8, lats), f32), ((feats + 8, lats), f32)],
        grad, enc_both, own_ones,
    )
    far = lax.ppermute(away, "c", SWAP)
    came = lax.all_to_all(sent.astype(f16).reshape(PEERS, rows, LANES), PLANE, 0, 0, tiled=True)
    grad_in, grad_enc, grad_bias = call(
        finish,
        [((rows, S, feats), f32), ((feats, lats), f32), ((1, lats), f32)],
        came.astype(f32).reshape(wide, LANES), keep, far,
    )
    return (grad_enc, grad_bias[0], grad_in)


def solution(mesh):
    fine = Mesh(mesh.devices.reshape(YL, Z, C, YH, X), AXES)
    return jax.shard_map(
        local,
        mesh=fine,
        in_specs=(
            P(LAT, None, TGT),
            P(TGT, LAT),
            P(LAT),
            P(None, LAT),
            P(TGT, LAT, None),
            P(TGT, LAT, None),
            P(),
        ),
        out_specs=(P(TGT, LAT), P(LAT), P(LAT, None, TGT)),
        check_vma=False,
    )
```
